256 devices in a mesh: seq: 128 (over z, y, x), head: 2 (over core).
Axes of the slice: x: 4, y: 4, z: 8, core: 2. Of those that a mesh axis runs over, the one named last changes fastest.
Arguments:
- input_rows: bfloat16 [32768, 4096], P(('seq', 'head')), may hold values from -40 to 40
- doc_lengths: int32 [64], replicated, may hold values from 1 to 1024, 32768 in all
- w_query: bfloat16 [4096, 4096], P(None, 'head'), may hold values from -0.09375 to 0.09375
- key_weight: bfloat16 [4096, 1024], P(None, 'head'), may hold values from -0.09375 to 0.09375
- value_weight: bfloat16 [4096, 1024], P(None, 'head'), may hold values from -0.09375 to 0.09375
- w_out: bfloat16 [4096, 4096], P('head'), may hold values from -0.5 to 0.5
Outputs:
- mixed: bfloat16 [32768, 4096], P(('seq', 'head'))
The draws below stay inside these ranges and needn't reach their ends.
All inputs are finite; a program needn't handle non-finite values.
Results may differ from the reference program's by a relative error of at most 0.013.
Values may be sent and summed in bfloat16 or wider, within the bound.
A program may use at most 192 MiB of HBM per device.

```python
import math
import jax
import jax.numpy as jnp
import numpy as np
from jax import lax

MODEL_WIDTH = 4096
QUERY_HEADS = 32
KEY_VALUE_HEADS = 8
HEAD_SIZE = 128
TOK_SEQ = 256
REACH = 4
WINDOW_TOKENS = 32768
DOC_MAX = 1024
DOCS = 64
N_SEQ = 128


def draw_input_rows(key, part):
    first = jax.random.fold_in(key, 0)
    base = jax.random.normal(first, (WINDOW_TOKENS, MODEL_WIDTH), jnp.float32)
    return jnp.clip(base, -6.0, 6.0).astype(jnp.bfloat16)


def steps_of(own_key, dims, cuts, low, largest):
    loudness = 1.0
    for position, shards_of in cuts:
        heights = jax.random.uniform(jax.random.fold_in(jax.random.fold_in(own_key, 6), position), (shards_of,), jnp.float32, low / len(cuts), largest / len(cuts))
        loudness = loudness * jnp.repeat(jnp.exp(heights), dims[position] // shards_of).reshape((-1,) + (1,) * (len(dims) - 1 - position))
    return loudness


def profile(count, total, most, slope):
    loads = [(1 << 20) // math.isqrt(grade ** slope) + 1 for grade in range(2, count + 1)]
    rest, given = total - most - (count - 1), [1] * (count - 1)
    while rest > 0:
        free = [i for i in range(count - 1) if given[i] < most]
        pool, budget = sum([loads[i] for i in free]), rest
        for i in free:
            more = min(most - given[i], max(1, budget * loads[i] // pool), rest)
            given[i] = given[i] + more
            rest = rest - more
    return np.array([most] + given)


def uneven_parts(key, number_of, total, reach, slope):
    if number_of == 2:
        one = jax.random.randint(key, (), max(1, total - reach), min(reach, total - 1) + 1)
        return jnp.stack([one, total - one])
    sizes = jnp.asarray(profile(number_of, total, reach, slope), jnp.int32)
    twos = (number_of - 1) // 2
    giver, sink = sizes[1:1 + 2 * twos:2], sizes[2:2 + 2 * twos:2]
    room = jnp.minimum(giver - 1, reach - sink)
    moved = jax.random.randint(jax.random.fold_in(key, 1), (twos,), 0, 1 << 20) % (room + 1)
    sizes = sizes.at[1:1 + 2 * twos:2].set(giver - moved).at[2:2 + 2 * twos:2].set(sink + moved)
    return sizes[jax.random.permutation(jax.random.fold_in(key, 2), number_of)]


def centred(own_key, shape, deviation, limit, pieces=(), held_as=jnp.bfloat16):
    entries = jax.random.normal(own_key, shape, jnp.float32) * deviation
    if len(pieces) > 0:
        entries = steps_of(own_key, shape, pieces, -0.22, 0.18) * entries
    return jnp.clip(entries, min=-limit, max=limit).astype(held_as)


def setup_inputs(seed: int = 0) -> dict:
    arg_keys = jax.random.split(jax.random.key(seed), 7)
    return {
        "input_rows": draw_input_rows(jax.random.fold_in(arg_keys[6], 71), 0),
        "doc_lengths": uneven_parts(arg_keys[1], DOCS, WINDOW_TOKENS, DOC_MAX, 2).astype(jnp.int32),
        "w_query": centred(arg_keys[2], (MODEL_WIDTH, QUERY_HEADS * HEAD_SIZE), MODEL_WIDTH ** -0.5, 0.09375, ((1, 2),)),
        "key_weight": centred(arg_keys[3], (MODEL_WIDTH, KEY_VALUE_HEADS * HEAD_SIZE), MODEL_WIDTH ** -0.5, 0.09375, ((1, 2),)),
        "value_weight": centred(arg_keys[4], (MODEL_WIDTH, KEY_VALUE_HEADS * HEAD_SIZE), MODEL_WIDTH ** -0.5, 0.09375, ((1, 2),)),
        "w_out": centred(arg_keys[5], (QUERY_HEADS * HEAD_SIZE, MODEL_WIDTH), HEAD_SIZE ** -0.5, 0.5, ((0, 2),)),
    }


NEG_FILL = -1.0e30


def inverse_frequency():
    table = []
    for number in range(HEAD_SIZE // 2):
        base_freq = 500000.0 ** (-(2.0 * number) / HEAD_SIZE)
        wavelength = 2.0 * math.pi / base_freq
        smooth = (8192.0 / wavelength - 1.0) / 3.0
        if wavelength < 2048.0:
            table.append(base_freq)
        elif wavelength > 8192.0:
            table.append(base_freq / 8.0)
        else:
            table.append((1.0 - smooth) * base_freq / 8.0 + smooth * base_freq)
    return jnp.asarray(table, dtype=jnp.float32)


def rotate(value_matrix, cosine, sine_table):
    half_size = value_matrix.shape[-1] // 2
    first = value_matrix[..., :half_size]
    second = value_matrix[..., half_size:]
    return jnp.concatenate([first * cosine - second * sine_table, second * cosine + first * sine_table], axis=-1)


def reference(input_rows, doc_lengths, w_query, key_weight, value_weight, w_out):
    positions = jnp.arange(WINDOW_TOKENS, dtype=jnp.int32)
    doc_ends = jnp.cumsum(doc_lengths).astype(jnp.int32)
    doc_ids = jnp.sum((positions[:, None] >= doc_ends[None, :]).astype(jnp.int32), axis=1).astype(jnp.int32)
    angles = positions.astype(jnp.float32)[:, None] * inverse_frequency()[None, :]
    cosine = jnp.cos(angles)[:, None, :]
    sine_table = jnp.sin(angles)[:, None, :]
    query_matrix = jnp.dot(input_rows, w_query, preferred_element_type=jnp.float32).reshape(WINDOW_TOKENS, QUERY_HEADS, HEAD_SIZE)
    query_matrix = rotate(query_matrix, cosine, sine_table).astype(jnp.bfloat16)
    key_matrix = jnp.dot(input_rows, key_weight, preferred_element_type=jnp.float32).reshape(WINDOW_TOKENS, KEY_VALUE_HEADS, HEAD_SIZE)
    key_matrix = rotate(key_matrix, cosine, sine_table).astype(jnp.bfloat16)
    value_matrix = jnp.dot(input_rows, value_weight, preferred_element_type=jnp.float32).astype(jnp.bfloat16).reshape(WINDOW_TOKENS, KEY_VALUE_HEADS, HEAD_SIZE)
    query_group = QUERY_HEADS // KEY_VALUE_HEADS
    grouped_queries = query_matrix.reshape(WINDOW_TOKENS, KEY_VALUE_HEADS, query_group, HEAD_SIZE)
    span = (REACH + 1) * TOK_SEQ
    scale = HEAD_SIZE ** -0.5

    def block(index):
        index = index.astype(jnp.int32)
        q_start = index * TOK_SEQ
        k_start = (jnp.clip(index - REACH, 0, N_SEQ - REACH - 1) * TOK_SEQ).astype(jnp.int32)
        q_block = lax.dynamic_slice_in_dim(grouped_queries, q_start, TOK_SEQ, 0).astype(jnp.float32)
        k_block = lax.dynamic_slice_in_dim(key_matrix, k_start, span, 0).astype(jnp.float32)
        v_block = lax.dynamic_slice_in_dim(value_matrix, k_start, span, 0).astype(jnp.float32)
        q_pos = q_start + jnp.arange(TOK_SEQ, dtype=jnp.int32)
        k_pos = k_start + jnp.arange(span, dtype=jnp.int32)
        q_doc = lax.dynamic_slice_in_dim(doc_ids, q_start, TOK_SEQ, 0)
        k_doc = lax.dynamic_slice_in_dim(doc_ids, k_start, span, 0)
        scores = jnp.einsum("tkgd,skd->kgts", q_block, k_block) * scale
        allowed = (q_doc[:, None] == k_doc[None, :]) & (k_pos[None, :] <= q_pos[:, None])
        scores = jnp.where(allowed, scores, NEG_FILL)
        row_max = jnp.max(scores, axis=-1, keepdims=True)
        weights = jnp.where(allowed, jnp.exp(scores - row_max), 0.0)
        totals = jnp.sum(weights, axis=-1)
        rounded = lax.optimization_barrier(weights.astype(jnp.bfloat16)).astype(jnp.float32)
        output = jnp.einsum("kgts,skd->kgtd", rounded, v_block) / totals[..., None]
        return output.transpose(2, 0, 1, 3).reshape(TOK_SEQ, QUERY_HEADS * HEAD_SIZE).astype(jnp.bfloat16)

    blocks = lax.map(block, jnp.arange(N_SEQ, dtype=jnp.int32))
    attended = blocks.reshape(WINDOW_TOKENS, QUERY_HEADS * HEAD_SIZE)
    return jnp.dot(attended, w_out, preferred_element_type=jnp.float32).astype(jnp.bfloat16)
```

```python
import math

import jax
import jax.numpy as jnp
import numpy as np
from jax import lax
from jax.experimental import pallas as pl
from jax.experimental.pallas import tpu as pltpu
from jax.sharding import PartitionSpec as P

MESH = pl.DeviceIdType.MESH
HEAD_SIZE = 128
TOK = 256
HALF = 128
WIDTH = 4096
KV_HERE = 4
GROUP = 4
SLOTS = 5
X_RING = 4
N_SEQ = 128
DOCS = 64
NEG_FILL = -1e30
COLS = 512
CHUNKS = WIDTH // COLS

TO_Y, TO_RIGHT, TO_LEFT, ON_RIGHT, ON_LEFT, ON_Y = range(6)
AT4, AT1, AT3, AT2K, AT2V, ATT = range(6)


def inverse_frequency():
    table = []
    for number in range(HEAD_SIZE // 2):
        base_freq = 500000.0 ** (-(2.0 * number) / HEAD_SIZE)
        wavelength = 2.0 * math.pi / base_freq
        smooth = (8192.0 / wavelength - 1.0) / 3.0
        if wavelength < 2048.0:
            table.append(base_freq)
        elif wavelength > 8192.0:
            table.append(base_freq / 8.0)
        else:
            table.append((1.0 - smooth) * base_freq / 8.0 + smooth * base_freq)
    return np.asarray(table, dtype=np.float32).astype(np.float64)


def rotary_tables():
    freq = np.concatenate([inverse_frequency()] * 2)
    rows = np.arange(TOK)[:, None] * freq
    starts = (np.arange(N_SEQ) * TOK)[:, None] * freq
    return np.concatenate(
        [np.cos(rows), np.sin(rows), np.cos(starts), np.sin(starts)]
    ).astype(np.float32)


def kernel(
    x_hbm, docs, wq_hbm, wk_hbm, wv_hbm, wo_hbm, tab_hbm,
    out,
    x, wkv, wq, wo, q, kv, acc, send, recv, att, bias, tab, rope,
    x_sem, wkv_sem, wq_sem, wo_sem, tab_sem,
    xs_sem, xr_sem, kv_send, kv_recv, red_send, red_recv,
):
    seq = lax.axis_index("seq")
    head = lax.axis_index("head")
    other = 1 - head
    place = lax.rem(seq, X_RING)
    right = jnp.where(place == X_RING - 1, seq - (X_RING - 1), seq + 1)
    left = jnp.where(place == 0, seq + (X_RING - 1), seq - 1)
    later = lax.rem(seq + X_RING, N_SEQ)
    earlier = lax.rem(seq + N_SEQ - X_RING, N_SEQ)
    own_rows = pl.ds(pl.multiple_of(head * HALF, HALF), HALF)
    other_rows = pl.ds(pl.multiple_of(other * HALF, HALF), HALF)

    x_copy = pltpu.make_async_copy(x_hbm, x.at[own_rows, :], x_sem)
    tab_copy = pltpu.make_async_copy(tab_hbm, tab, tab_sem)

    def lanes(number, size):
        return pl.ds(pl.multiple_of(number * size, size), size)

    def wkv_copies(h):
        return (
            pltpu.make_async_copy(
                wk_hbm.at[:, lanes(h, HEAD_SIZE)], wkv.at[h, :, pl.ds(0, HEAD_SIZE)], wkv_sem.at[h, 0]
            ),
            pltpu.make_async_copy(
                wv_hbm.at[:, lanes(h, HEAD_SIZE)],
                wkv.at[h, :, pl.ds(HEAD_SIZE, HEAD_SIZE)],
                wkv_sem.at[h, 1],
            ),
        )

    def wq_copy(h):
        return pltpu.make_async_copy(
            wq_hbm.at[:, lanes(h, GROUP * HEAD_SIZE)], wq.at[h], wq_sem.at[h]
        )

    def wo_copy(h):
        return pltpu.make_async_copy(
            wo_hbm.at[lanes(h, GROUP * HEAD_SIZE), :], wo.at[h], wo_sem.at[h]
        )

    x_copy.start()
    tab_copy.start()
    for h in range(KV_HERE):
        for copy in wkv_copies(h):
            copy.start()

    barrier = pltpu.get_barrier_semaphore()
    for target in ((seq, other), (right, head), (left, head), (later, head), (earlier, head)):
        pl.semaphore_signal(barrier, inc=1, device_id=target, device_id_type=MESH)
    pl.semaphore_wait(barrier, 5)

    def x_exchange():
        return pltpu.make_async_remote_copy(
            src_ref=x_hbm,
            dst_ref=x.at[own_rows, :],
            send_sem=xs_sem,
            recv_sem=xr_sem,
            device_id=(seq, other),
            device_id_type=MESH,
        )

    x_exchange().start()

    base = seq * TOK
    position = base + lax.broadcasted_iota(jnp.int32, (8, TOK), 1)

    def next_doc(number, state):
        end, start = state
        end = end + docs[number]
        return end, jnp.where(end <= position, end, start)

    _, start_row = lax.fori_loop(
        0, DOCS, next_doc, (jnp.int32(0), jnp.zeros((8, TOK), jnp.int32))
    )
    start_row = start_row.astype(jnp.float32)
    start = jnp.transpose(jnp.concatenate([start_row] * (HEAD_SIZE // 8), axis=0))
    base_f = base.astype(jnp.float32)
    lane = lax.broadcasted_iota(jnp.int32, (TOK, HEAD_SIZE), 1)
    row = lax.broadcasted_iota(jnp.int32, (TOK, HEAD_SIZE), 0)
    for slot in range(SLOTS):
        for half in range(TOK // HEAD_SIZE):
            offset = lane + half * HEAD_SIZE
            allowed = offset.astype(jnp.float32) + (base_f - float(slot * TOK)) >= start
            if slot == 0:
                allowed = allowed & (offset <= row)
            bias[:, pl.ds(slot * TOK + half * HEAD_SIZE, HEAD_SIZE)] = jnp.where(
                allowed, 0.0, NEG_FILL
            )

    tab_copy.wait()
    cos_row, sin_row = tab[pl.ds(0, TOK), :], tab[pl.ds(TOK, TOK), :]
    cos_base = tab[pl.ds(2 * TOK + seq, 1), :]
    sin_base = tab[pl.ds(2 * TOK + N_SEQ + seq, 1), :]
    cosine = cos_row * cos_base - sin_row * sin_base
    sine = sin_row * cos_base + cos_row * sin_base
    sine = jnp.where(lane < HEAD_SIZE // 2, -sine, sine)
    scale = HEAD_SIZE ** (-0.5) * math.log2(math.e)
    rope[0] = cosine
    rope[1] = sine
    rope[2] = cosine * scale
    rope[3] = sine * scale

    def rotated(value, which):
        turned = pltpu.roll(value, HEAD_SIZE // 2, 1)
        return (value * rope[which] + turned * rope[which + 1]).astype(jnp.bfloat16)

    def block(h, slot):
        return kv.at[:, h, lanes(slot, TOK), :]

    def part(which, h, slot):
        return kv.at[which, h, lanes(slot, TOK), :]

    def remote(source, target, h, sending, receiving, device):
        return pltpu.make_async_remote_copy(
            src_ref=source,
            dst_ref=target,
            send_sem=kv_send.at[h, sending],
            recv_sem=kv_recv.at[h, receiving],
            device_id=(device, head),
            device_id_type=MESH,
        )

    def to_later(h):
        return remote(block(h, 0), block(h, 4), h, TO_Y, AT4, later)

    def to_right(h, slot):
        return remote(block(h, slot), block(h, 1), h, TO_RIGHT, AT1, right)

    def to_left(h, slot):
        return remote(block(h, slot), block(h, 3), h, TO_LEFT, AT3, left)

    last = place == X_RING - 1
    first = place == 0

    def on_right(h):
        return remote(
            part(0, h, 1), part(0, h, jnp.where(last, 5, 2)), h, ON_RIGHT,
            jnp.where(last, ATT, AT2K), right,
        )

    def on_left(h):
        return remote(
            part(1, h, 3), part(1, h, jnp.where(first, 5, 2)), h, ON_LEFT,
            jnp.where(first, ATT, AT2V), left,
        )

    def key_on_later(h):
        return remote(part(0, h, 5), part(0, h, 2), h, ON_Y, AT2K, later)

    def value_on_earlier(h):
        return remote(part(1, h, 5), part(1, h, 2), h, ON_Y, AT2V, earlier)

    def stage_a(h):
        to_later(h).start()

        @pl.when(jnp.logical_not(last))
        def _():
            to_right(h, 0).start()

        @pl.when(first)
        def _():
            to_left(h, 0).start()

    def stage_b(h):
        to_later(h).wait_recv()

        @pl.when(last)
        def _():
            to_right(h, 4).start()

        @pl.when(jnp.logical_not(first))
        def _():
            to_left(h, 4).start()

    def stage_c(h):
        to_right(h, 0).wait_recv()
        on_right(h).start()
        to_left(h, 0).wait_recv()
        on_left(h).start()

    def stage_d(h):
        @pl.when(first)
        def _():
            remote(part(0, h, 5), part(0, h, 5), h, ON_Y, ATT, later).wait_recv()
            key_on_later(h).start()

        @pl.when(last)
        def _():
            remote(part(1, h, 5), part(1, h, 5), h, ON_Y, ATT, earlier).wait_recv()
            value_on_earlier(h).start()

    x_copy.wait()
    x_exchange().wait()

    def project_kv(h, carry):
        for copy in wkv_copies(h):
            copy.wait()
        wq_copy(h).start()
        both = jnp.dot(x[...], wkv[h], preferred_element_type=jnp.float32)
        kv[0, h, pl.ds(0, TOK), :] = rotated(both[:, :HEAD_SIZE], 0)
        kv[1, h, pl.ds(0, TOK), :] = both[:, HEAD_SIZE:].astype(jnp.bfloat16)
        stage_a(h)
        return carry

    lax.fori_loop(0, KV_HERE, project_kv, 0)

    def project_q(h, carry):
        wq_copy(h).wait()
        wo_copy(h).start()
        some = jnp.dot(x[...], wq[h], preferred_element_type=jnp.float32)
        for number in range(GROUP):
            q[h * GROUP + number] = rotated(
                some[:, number * HEAD_SIZE : (number + 1) * HEAD_SIZE], 2
            )
        stage_b(h)

        @pl.when(h >= 1)
        def _():
            stage_c(h - 1)

        @pl.when(h >= 2)
        def _():
            stage_d(h - 2)

        return carry

    lax.fori_loop(0, KV_HERE, project_q, 0)
    stage_c(KV_HERE - 1)
    stage_d(KV_HERE - 2)
    stage_d(KV_HERE - 1)

    def reduce_copy(chunk):
        return pltpu.make_async_remote_copy(
            src_ref=send.at[chunk],
            dst_ref=recv.at[chunk],
            send_sem=red_send.at[chunk],
            recv_sem=red_recv.at[chunk],
            device_id=(seq, other),
            device_id_type=MESH,
        )

    acc[...] = jnp.zeros_like(acc)

    def attend(h, carry):
        remote(part(0, h, 2), part(0, h, 2), h, ON_Y, AT2K, later).wait_recv()
        remote(part(1, h, 2), part(1, h, 2), h, ON_Y, AT2V, later).wait_recv()

        def one_head(number, inner):
            keys = kv[0, h, pl.ds(0, SLOTS * TOK), :]
            values = kv[1, h, pl.ds(0, SLOTS * TOK), :]
            values = jnp.concatenate([values, jnp.ones_like(values)], axis=1)
            score = lax.dot_general(
                q[h * GROUP + number], keys, (((1,), (1,)), ((), ())),
                preferred_element_type=jnp.float32,
            )
            score = score + bias[...]
            rowmax = jnp.max(score, axis=1, keepdims=True)
            weight = jnp.exp2(score - rowmax).astype(jnp.bfloat16)
            mixed = jnp.dot(weight, values, preferred_element_type=jnp.float32)
            att[:, lanes(number, HEAD_SIZE)] = (
                mixed[:, :HEAD_SIZE] / mixed[:, HEAD_SIZE:]
            ).astype(jnp.bfloat16)
            return inner

        lax.fori_loop(0, GROUP, one_head, 0)
        wo_copy(h).wait()

        def project_out(chunk, inner):
            columns = lanes(chunk, COLS)
            acc[:, columns] += jnp.dot(
                att[...], wo[h, :, columns], preferred_element_type=jnp.float32
            )

            @pl.when(h == KV_HERE - 1)
            def _():
                send[chunk] = acc[other_rows, columns].astype(jnp.bfloat16)
                reduce_copy(chunk).start()

            return inner

        lax.fori_loop(0, CHUNKS, project_out, 0)
        return carry

    lax.fori_loop(0, KV_HERE, attend, 0)

    def finish(chunk, carry):
        columns = lanes(chunk, COLS)
        reduce_copy(chunk).wait()
        out[:, columns] = (
            acc[own_rows, columns] + recv[chunk].astype(jnp.float32)
        ).astype(jnp.bfloat16)
        return carry

    lax.fori_loop(0, CHUNKS, finish, 0)

    def sent(h, carry):
        to_later(h).wait_send()
        to_right(h, 0).wait_send()
        to_left(h, 0).wait_send()
        on_right(h).wait_send()
        on_left(h).wait_send()

        @pl.when(first)
        def _():
            key_on_later(h).wait_send()

        @pl.when(last)
        def _():
            value_on_earlier(h).wait_send()

        return carry

    lax.fori_loop(0, KV_HERE, sent, 0)


def body(input_rows, doc_lengths, w_query, key_weight, value_weight, w_out):
    table = jnp.asarray(rotary_tables())
    hbm = pl.BlockSpec(memory_space=pl.ANY)
    dma = pltpu.SemaphoreType.DMA
    wide = GROUP * HEAD_SIZE
    return pl.pallas_call(
        kernel,
        out_shape=jax.ShapeDtypeStruct((HALF, WIDTH), jnp.bfloat16),
        in_specs=[hbm, pl.BlockSpec(memory_space=pltpu.SMEM), hbm, hbm, hbm, hbm, hbm],
        out_specs=pl.BlockSpec(memory_space=pltpu.VMEM),
        scratch_shapes=[
            pltpu.VMEM((TOK, WIDTH), jnp.bfloat16),
            pltpu.VMEM((KV_HERE, WIDTH, 2 * HEAD_SIZE), jnp.bfloat16),
            pltpu.VMEM((KV_HERE, WIDTH, wide), jnp.bfloat16),
            pltpu.VMEM((KV_HERE, wide, WIDTH), jnp.bfloat16),
            pltpu.VMEM((KV_HERE * GROUP, TOK, HEAD_SIZE), jnp.bfloat16),
            pltpu.VMEM((2, KV_HERE, (SLOTS + 1) * TOK, HEAD_SIZE), jnp.bfloat16),
            pltpu.VMEM((TOK, WIDTH), jnp.float32),
            pltpu.VMEM((CHUNKS, HALF, COLS), jnp.bfloat16),
            pltpu.VMEM((CHUNKS, HALF, COLS), jnp.bfloat16),
            pltpu.VMEM((TOK, wide), jnp.bfloat16),
            pltpu.VMEM((TOK, SLOTS * TOK), jnp.float32),
            pltpu.VMEM((2 * TOK + 2 * N_SEQ, HEAD_SIZE), jnp.float32),
            pltpu.VMEM((4, TOK, HEAD_SIZE), jnp.float32),
            dma(()), dma((KV_HERE, 2)), dma((KV_HERE,)), dma((KV_HERE,)), dma(()),
            dma(()), dma(()), dma((KV_HERE, 6)), dma((KV_HERE, 6)), dma((CHUNKS,)), dma((CHUNKS,)),
        ],
        compiler_params=pltpu.CompilerParams(
            collective_id=0, has_side_effects=True, vmem_limit_bytes=62 << 20
        ),
        name="layer",
    )(input_rows, doc_lengths, w_query, key_weight, value_weight, w_out, table)


def solution(mesh):
    in_specs = (
        P(("seq", "head"), None),
        P(),
        P(None, "head"),
        P(None, "head"),
        P(None, "head"),
        P("head", None),
    )
    out_specs = P(("seq", "head"), None)
    return jax.shard_map(body, mesh=mesh, in_specs=in_specs, out_specs=out_specs, check_vma=False)
```

```python
import math

import jax
import jax.numpy as jnp
import numpy as np
from jax import lax
from jax.experimental import pallas as pl
from jax.experimental.pallas import tpu as pltpu
from jax.sharding import PartitionSpec as P

MESH = pl.DeviceIdType.MESH
HEAD_SIZE = 128
TOK = 256
HALF = 128
WIDTH = 4096
KV_HERE = 4
GROUP = 4
SLOTS = 5
X_RING = 4
N_SEQ = 128
DOCS = 64
NEG_FILL = -1e30
COLS = 1024
CHUNKS = WIDTH // COLS
WIDE_COLS = 2048

TO_Y, TO_RIGHT, TO_LEFT, ON_RIGHT, ON_LEFT, ON_Y = range(6)
AT4, AT1, AT3, AT2K, AT2V, ATT = range(6)


def inverse_frequency():
    table = []
    for number in range(HEAD_SIZE // 2):
        base_freq = 500000.0 ** (-(2.0 * number) / HEAD_SIZE)
        wavelength = 2.0 * math.pi / base_freq
        smooth = (8192.0 / wavelength - 1.0) / 3.0
        if wavelength < 2048.0:
            table.append(base_freq)
        elif wavelength > 8192.0:
            table.append(base_freq / 8.0)
        else:
            table.append((1.0 - smooth) * base_freq / 8.0 + smooth * base_freq)
    return np.asarray(table, dtype=np.float32).astype(np.float64)


def rotary_tables():
    freq = np.concatenate([inverse_frequency()] * 2)
    rows = np.arange(TOK)[:, None] * freq
    starts = (np.arange(N_SEQ) * TOK)[:, None] * freq
    return np.concatenate(
        [np.cos(rows), np.sin(rows), np.cos(starts), np.sin(starts)]
    ).astype(np.float32)


def kernel(
    x_hbm, docs, wq_hbm, wk_hbm, wv_hbm, wo_hbm, tab_hbm,
    out,
    x, wkv, wq, wo, q, kv, acc, send, recv, att, bias, tab, rope,
    x_sem, wkv_sem, wq_sem, wo_sem, tab_sem,
    xs_sem, xr_sem, kv_send, kv_recv, red_send, red_recv,
):
    seq = lax.axis_index("seq")
    head = lax.axis_index("head")
    other = 1 - head
    place = lax.rem(seq, X_RING)
    right = jnp.where(place == X_RING - 1, seq - (X_RING - 1), seq + 1)
    left = jnp.where(place == 0, seq + (X_RING - 1), seq - 1)
    has_later = seq < N_SEQ - X_RING
    has_earlier = seq >= X_RING
    later = jnp.where(has_later, seq + X_RING, seq)
    earlier = jnp.where(has_earlier, seq - X_RING, seq)
    gives_far = seq == N_SEQ - 3
    takes_far = seq == N_SEQ - 1
    own_rows = pl.ds(pl.multiple_of(head * HALF, HALF), HALF)
    other_rows = pl.ds(pl.multiple_of(other * HALF, HALF), HALF)

    x_copy = pltpu.make_async_copy(x_hbm, x.at[own_rows, :], x_sem)
    tab_copy = pltpu.make_async_copy(tab_hbm, tab, tab_sem)

    def lanes(number, size):
        return pl.ds(pl.multiple_of(number * size, size), size)

    def wkv_copies(h):
        return (
            pltpu.make_async_copy(
                wk_hbm.at[:, lanes(h, HEAD_SIZE)], wkv.at[h, :, pl.ds(0, HEAD_SIZE)], wkv_sem.at[h, 0]
            ),
            pltpu.make_async_copy(
                wv_hbm.at[:, lanes(h, HEAD_SIZE)],
                wkv.at[h, :, pl.ds(HEAD_SIZE, HEAD_SIZE)],
                wkv_sem.at[h, 1],
            ),
        )

    def wq_copy(h):
        return pltpu.make_async_copy(
            wq_hbm.at[:, lanes(h, GROUP * HEAD_SIZE)], wq.at[h], wq_sem.at[h]
        )

    def wo_copy(h):
        return pltpu.make_async_copy(
            wo_hbm.at[lanes(h, GROUP * HEAD_SIZE), :], wo.at[h], wo_sem.at[h]
        )

    x_copy.start()
    tab_copy.start()
    for h in range(KV_HERE):
        for copy in wkv_copies(h):
            copy.start()

    barrier = pltpu.get_barrier_semaphore()

    def greet(target):
        pl.semaphore_signal(barrier, inc=1, device_id=target, device_id_type=MESH)

    for target in ((seq, other), (right, head), (left, head)):
        greet(target)

    @pl.when(has_later)
    def _():
        greet((later, head))

    @pl.when(has_earlier)
    def _():
        greet((earlier, head))

    @pl.when(gives_far)
    def _():
        greet((seq + 2, head))

    @pl.when(takes_far)
    def _():
        greet((seq - 2, head))

    callers = 3 + has_later.astype(jnp.int32) + has_earlier.astype(jnp.int32)
    callers = callers + gives_far.astype(jnp.int32) + takes_far.astype(jnp.int32)
    pl.semaphore_wait(barrier, callers)

    def x_exchange():
        return pltpu.make_async_remote_copy(
            src_ref=x_hbm,
            dst_ref=x.at[own_rows, :],
            send_sem=xs_sem,
            recv_sem=xr_sem,
            device_id=(seq, other),
            device_id_type=MESH,
        )

    x_exchange().start()

    base = seq * TOK
    position = base + lax.broadcasted_iota(jnp.int32, (8, TOK), 1)

    def next_doc(number, state):
        end, start = state
        end = end + docs[number]
        return end, jnp.where(end <= position, end, start)

    _, start_row = lax.fori_loop(
        0, DOCS, next_doc, (jnp.int32(0), jnp.zeros((8, TOK), jnp.int32))
    )
    start_row = start_row.astype(jnp.float32)
    start = jnp.transpose(jnp.concatenate([start_row] * (HEAD_SIZE // 8), axis=0))
    base_f = base.astype(jnp.float32)
    lane = lax.broadcasted_iota(jnp.int32, (TOK, HEAD_SIZE), 1)
    row = lax.broadcasted_iota(jnp.int32, (TOK, HEAD_SIZE), 0)
    for slot in range(SLOTS):
        for half in range(TOK // HEAD_SIZE):
            offset = lane + half * HEAD_SIZE
            allowed = offset.astype(jnp.float32) + (base_f - float(slot * TOK)) >= start
            if slot == 0:
                allowed = allowed & (offset <= row)
            bias[:, pl.ds(slot * TOK + half * HEAD_SIZE, HEAD_SIZE)] = jnp.where(
                allowed, 0.0, NEG_FILL
            )

    tab_copy.wait()
    cos_row, sin_row = tab[pl.ds(0, TOK), :], tab[pl.ds(TOK, TOK), :]
    cos_base = tab[pl.ds(2 * TOK + seq, 1), :]
    sin_base = tab[pl.ds(2 * TOK + N_SEQ + seq, 1), :]
    cosine = cos_row * cos_base - sin_row * sin_base
    sine = sin_row * cos_base + cos_row * sin_base
    sine = jnp.where(lane < HEAD_SIZE // 2, -sine, sine)
    scale = HEAD_SIZE ** (-0.5) * math.log2(math.e)
    rope[0] = cosine
    rope[1] = sine
    rope[2] = cosine * scale
    rope[3] = sine * scale

    def rotated(value, which):
        turned = pltpu.roll(value, HEAD_SIZE // 2, 1)
        return (value * rope[which] + turned * rope[which + 1]).astype(jnp.bfloat16)

    def block(h, slot):
        return kv.at[:, h, lanes(slot, TOK), :]

    def part(which, h, slot):
        return kv.at[which, h, lanes(slot, TOK), :]

    def remote(source, target, h, sending, receiving, device):
        return pltpu.make_async_remote_copy(
            src_ref=source,
            dst_ref=target,
            send_sem=kv_send.at[h, sending],
            recv_sem=kv_recv.at[h, receiving],
            device_id=(device, head),
            device_id_type=MESH,
        )

    def to_later(h):
        return remote(block(h, 0), block(h, 4), h, TO_Y, AT4, later)

    def to_right(h, slot):
        return remote(block(h, slot), block(h, 1), h, TO_RIGHT, AT1, right)

    def to_left(h, slot):
        return remote(block(h, slot), block(h, 3), h, TO_LEFT, AT3, left)

    last = place == X_RING - 1
    first = place == 0

    def on_right(h):
        return remote(
            part(0, h, 1), part(0, h, jnp.where(last, 5, 2)), h, ON_RIGHT,
            jnp.where(last, ATT, AT2K), right,
        )

    def on_left(h):
        return remote(
            part(1, h, 3), part(1, h, jnp.where(first, 5, 2)), h, ON_LEFT,
            jnp.where(first, ATT, AT2V), left,
        )

    def key_on_later(h):
        return remote(part(0, h, 5), part(0, h, 2), h, ON_Y, AT2K, later)

    def value_on_earlier(h):
        return remote(part(1, h, 5), part(1, h, 2), h, ON_Y, AT2V, earlier)

    def value_far(h):
        return remote(part(1, h, 0), part(1, h, 2), h, ON_Y, AT2V, seq + 2)

    def stage_a(h):
        @pl.when(has_later)
        def _():
            to_later(h).start()

        @pl.when(gives_far)
        def _():
            value_far(h).start()

        @pl.when(jnp.logical_not(last))
        def _():
            to_right(h, 0).start()

        @pl.when(first)
        def _():
            to_left(h, 0).start()

    def stage_b(h):
        @pl.when(has_earlier)
        def _():
            to_later(h).wait_recv()

        @pl.when(last)
        def _():
            to_right(h, 4).start()

        @pl.when(jnp.logical_not(first))
        def _():
            to_left(h, 4).start()

    def stage_c(h):
        to_right(h, 0).wait_recv()
        on_right(h).start()
        to_left(h, 0).wait_recv()
        on_left(h).start()

    def stage_d(h):
        @pl.when(first)
        def _():
            remote(part(0, h, 5), part(0, h, 5), h, ON_Y, ATT, later).wait_recv()

            @pl.when(has_later)
            def _():
                key_on_later(h).start()

        @pl.when(last)
        def _():
            remote(part(1, h, 5), part(1, h, 5), h, ON_Y, ATT, earlier).wait_recv()

            @pl.when(has_earlier)
            def _():
                value_on_earlier(h).start()

    @pl.when(jnp.logical_not(has_earlier))
    def _():
        kv[:, :, pl.ds(4 * TOK, TOK), :] = jnp.zeros((2, KV_HERE, TOK, HEAD_SIZE), jnp.bfloat16)

    @pl.when(seq == 0)
    def _():
        kv[0, :, pl.ds(2 * TOK, TOK), :] = jnp.zeros((KV_HERE, TOK, HEAD_SIZE), jnp.bfloat16)

    x_copy.wait()
    x_exchange().wait()

    def project_kv(h, carry):
        for copy in wkv_copies(h):
            copy.wait()
        wq_copy(h).start()
        both = jnp.dot(x[...], wkv[h], preferred_element_type=jnp.float32)
        kv[0, h, pl.ds(0, TOK), :] = rotated(both[:, :HEAD_SIZE], 0)
        kv[1, h, pl.ds(0, TOK), :] = both[:, HEAD_SIZE:].astype(jnp.bfloat16)
        stage_a(h)
        return carry

    lax.fori_loop(0, KV_HERE, project_kv, 0)

    def project_q(h, carry):
        wq_copy(h).wait()
        wo_copy(h).start()
        some = jnp.dot(x[...], wq[h], preferred_element_type=jnp.float32)
        for number in range(GROUP):
            q[h * GROUP + number] = rotated(
                some[:, number * HEAD_SIZE : (number + 1) * HEAD_SIZE], 2
            )
        stage_b(h)

        @pl.when(h >= 1)
        def _():
            stage_c(h - 1)

        @pl.when(h >= 2)
        def _():
            stage_d(h - 2)

        return carry

    lax.fori_loop(0, KV_HERE, project_q, 0)
    stage_c(KV_HERE - 1)
    stage_d(KV_HERE - 2)
    stage_d(KV_HERE - 1)

    def reduce_copy(chunk):
        return pltpu.make_async_remote_copy(
            src_ref=send.at[chunk],
            dst_ref=recv.at[chunk],
            send_sem=red_send.at[chunk],
            recv_sem=red_recv.at[chunk],
            device_id=(seq, other),
            device_id_type=MESH,
        )

    acc[...] = jnp.zeros_like(acc)

    def attend(h, carry):
        @pl.when(seq > 0)
        def _():
            remote(part(0, h, 2), part(0, h, 2), h, ON_Y, AT2K, later).wait_recv()

        remote(part(1, h, 2), part(1, h, 2), h, ON_Y, AT2V, later).wait_recv()
        keys = kv[0, h, pl.ds(0, SLOTS * TOK), :]
        values = kv[1, h, pl.ds(0, SLOTS * TOK), :]
        values = jnp.concatenate([values, jnp.ones_like(values)], axis=1)
        for number in range(GROUP):
            score = lax.dot_general(
                q[h * GROUP + number], keys, (((1,), (1,)), ((), ())),
                preferred_element_type=jnp.float32,
            )
            score = score + bias[...]
            rowmax = jnp.max(score, axis=1, keepdims=True)
            weight = jnp.exp2(score - rowmax).astype(jnp.bfloat16)
            mixed = jnp.dot(weight, values, preferred_element_type=jnp.float32)
            att[:, number * HEAD_SIZE : (number + 1) * HEAD_SIZE] = (
                mixed[:, :HEAD_SIZE] / mixed[:, HEAD_SIZE:]
            ).astype(jnp.bfloat16)
        wo_copy(h).wait()

        def project_out(chunk, inner):
            columns = lanes(chunk, WIDE_COLS)
            acc[:, columns] += jnp.dot(
                att[...], wo[h, :, columns], preferred_element_type=jnp.float32
            )
            return inner

        @pl.when(h < KV_HERE - 1)
        def _():
            lax.fori_loop(0, WIDTH // WIDE_COLS, project_out, 0)

        return carry

    lax.fori_loop(0, KV_HERE, attend, 0)

    def project_last(chunk, carry):
        columns = lanes(chunk, COLS)
        acc[:, columns] += jnp.dot(
            att[...], wo[KV_HERE - 1, :, columns], preferred_element_type=jnp.float32
        )
        send[chunk] = acc[other_rows, columns].astype(jnp.bfloat16)
        reduce_copy(chunk).start()
        return carry

    lax.fori_loop(0, CHUNKS, project_last, 0)

    def finish(chunk, carry):
        columns = lanes(chunk, COLS)
        reduce_copy(chunk).wait()
        out[:, columns] = (
            acc[own_rows, columns] + recv[chunk].astype(jnp.float32)
        ).astype(jnp.bfloat16)
        return carry

    lax.fori_loop(0, CHUNKS, finish, 0)

    def sent(h, carry):
        @pl.when(has_later)
        def _():
            to_later(h).wait_send()

        @pl.when(gives_far)
        def _():
            value_far(h).wait_send()

        to_right(h, 0).wait_send()
        to_left(h, 0).wait_send()
        on_right(h).wait_send()
        on_left(h).wait_send()

        @pl.when(first & has_later)
        def _():
            key_on_later(h).wait_send()

        @pl.when(last & has_earlier)
        def _():
            value_on_earlier(h).wait_send()

        return carry

    lax.fori_loop(0, KV_HERE, sent, 0)


def body(input_rows, doc_lengths, w_query, key_weight, value_weight, w_out):
    table = jnp.asarray(rotary_tables())
    hbm = pl.BlockSpec(memory_space=pl.ANY)
    dma = pltpu.SemaphoreType.DMA
    wide = GROUP * HEAD_SIZE
    return pl.pallas_call(
        kernel,
        out_shape=jax.ShapeDtypeStruct((HALF, WIDTH), jnp.bfloat16),
        in_specs=[hbm, pl.BlockSpec(memory_space=pltpu.SMEM), hbm, hbm, hbm, hbm, hbm],
        out_specs=pl.BlockSpec(memory_space=pltpu.VMEM),
        scratch_shapes=[
            pltpu.VMEM((TOK, WIDTH), jnp.bfloat16),
            pltpu.VMEM((KV_HERE, WIDTH, 2 * HEAD_SIZE), jnp.bfloat16),
            pltpu.VMEM((KV_HERE, WIDTH, wide), jnp.bfloat16),
            pltpu.VMEM((KV_HERE, wide, WIDTH), jnp.bfloat16),
            pltpu.VMEM((KV_HERE * GROUP, TOK, HEAD_SIZE), jnp.bfloat16),
            pltpu.VMEM((2, KV_HERE, (SLOTS + 1) * TOK, HEAD_SIZE), jnp.bfloat16),
            pltpu.VMEM((TOK, WIDTH), jnp.float32),
            pltpu.VMEM((CHUNKS, HALF, COLS), jnp.bfloat16),
            pltpu.VMEM((CHUNKS, HALF, COLS), jnp.bfloat16),
            pltpu.VMEM((TOK, wide), jnp.bfloat16),
            pltpu.VMEM((TOK, SLOTS * TOK), jnp.float32),
            pltpu.VMEM((2 * TOK + 2 * N_SEQ, HEAD_SIZE), jnp.float32),
            pltpu.VMEM((4, TOK, HEAD_SIZE), jnp.float32),
            dma(()), dma((KV_HERE, 2)), dma((KV_HERE,)), dma((KV_HERE,)), dma(()),
            dma(()), dma(()), dma((KV_HERE, 6)), dma((KV_HERE, 6)), dma((CHUNKS,)), dma((CHUNKS,)),
        ],
        compiler_params=pltpu.CompilerParams(
            collective_id=0, has_side_effects=True, vmem_limit_bytes=62 << 20
        ),
        name="layer",
    )(input_rows, doc_lengths, w_query, key_weight, value_weight, w_out, table)


def solution(mesh):
    in_specs = (
        P(("seq", "head"), None),
        P(),
        P(None, "head"),
        P(None, "head"),
        P(None, "head"),
        P("head", None),
    )
    out_specs = P(("seq", "head"), None)
    return jax.shard_map(body, mesh=mesh, in_specs=in_specs, out_specs=out_specs, check_vma=False)
```

```python
import math

import jax
import jax.numpy as jnp
import numpy as np
from jax import lax
from jax.experimental import pallas as pl
from jax.experimental.pallas import tpu as pltpu
from jax.sharding import PartitionSpec as P

MESH = pl.DeviceIdType.MESH
HEAD_SIZE = 128
TOK = 256
HALF = 128
WIDTH = 4096
KV_HERE = 4
GROUP = 4
SLOTS = 5
X_RING = 4
N_SEQ = 128
DOCS = 64
NEG_FILL = -1e30
COLS = 1024
CHUNKS = WIDTH // COLS
WIDE_COLS = 2048

AT1, AT2, AT3, AT4 = 1, 2, 3, 4
UNITS = 2 * KV_HERE


def inverse_frequency():
    table = []
    for number in range(HEAD_SIZE // 2):
        base_freq = 500000.0 ** (-(2.0 * number) / HEAD_SIZE)
        wavelength = 2.0 * math.pi / base_freq
        smooth = (8192.0 / wavelength - 1.0) / 3.0
        if wavelength < 2048.0:
            table.append(base_freq)
        elif wavelength > 8192.0:
            table.append(base_freq / 8.0)
        else:
            table.append((1.0 - smooth) * base_freq / 8.0 + smooth * base_freq)
    return np.asarray(table, dtype=np.float32).astype(np.float64)


def rotary_tables():
    freq = np.concatenate([inverse_frequency()] * 2)
    rows = np.arange(TOK)[:, None] * freq
    starts = (np.arange(N_SEQ) * TOK)[:, None] * freq
    return np.concatenate(
        [np.cos(rows), np.sin(rows), np.cos(starts), np.sin(starts)]
    ).astype(np.float32)


def kernel(
    x_hbm, docs, wq_hbm, wk_hbm, wv_hbm, wo_hbm, tab_hbm,
    out,
    x, wkv, wq, wo, q, kv, acc, send, recv, att, bias, tab, rope,
    x_sem, wkv_sem, wq_sem, wo_sem, tab_sem,
    xs_sem, xr_sem, kv_send, kv_recv, red_send, red_recv,
):
    seq = lax.axis_index("seq")
    head = lax.axis_index("head")
    other = 1 - head
    place = lax.rem(seq, X_RING)
    right = jnp.where(place == X_RING - 1, seq - (X_RING - 1), seq + 1)
    left = jnp.where(place == 0, seq + (X_RING - 1), seq - 1)
    first = place == 0
    last = place == X_RING - 1
    low = place < X_RING // 2
    far = jnp.where(low, seq + 2, seq - 2)
    has_later = seq < N_SEQ - X_RING
    has_earlier = seq >= X_RING
    later = jnp.where(has_later, seq + X_RING, seq)
    earlier = jnp.where(has_earlier, seq - X_RING, seq)
    own_rows = pl.ds(pl.multiple_of(head * HALF, HALF), HALF)
    other_rows = pl.ds(pl.multiple_of(other * HALF, HALF), HALF)

    x_copy = pltpu.make_async_copy(x_hbm, x.at[own_rows, :], x_sem)
    tab_copy = pltpu.make_async_copy(tab_hbm, tab, tab_sem)

    def lanes(number, size):
        return pl.ds(pl.multiple_of(number * size, size), size)

    def wkv_copies(h):
        return (
            pltpu.make_async_copy(
                wk_hbm.at[:, lanes(h, HEAD_SIZE)], wkv.at[h, :, pl.ds(0, HEAD_SIZE)], wkv_sem.at[h, 0]
            ),
            pltpu.make_async_copy(
                wv_hbm.at[:, lanes(h, HEAD_SIZE)],
                wkv.at[h, :, pl.ds(HEAD_SIZE, HEAD_SIZE)],
                wkv_sem.at[h, 1],
            ),
        )

    def wq_copy(h):
        return pltpu.make_async_copy(
            wq_hbm.at[:, lanes(h, GROUP * HEAD_SIZE)], wq.at[h], wq_sem.at[h]
        )

    def wo_copy(h):
        return pltpu.make_async_copy(
            wo_hbm.at[lanes(h, GROUP * HEAD_SIZE), :], wo.at[h], wo_sem.at[h]
        )

    x_copy.start()
    tab_copy.start()
    for h in range(KV_HERE):
        for copy in wkv_copies(h):
            copy.start()

    barrier = pltpu.get_barrier_semaphore()

    def greet(target):
        pl.semaphore_signal(barrier, inc=1, device_id=target, device_id_type=MESH)

    for target in ((seq, other), (right, head), (left, head), (far, head)):
        greet(target)

    @pl.when(has_later)
    def _():
        greet((later, head))

    @pl.when(has_earlier)
    def _():
        greet((earlier, head))

    def x_exchange():
        return pltpu.make_async_remote_copy(
            src_ref=x_hbm,
            dst_ref=x.at[own_rows, :],
            send_sem=xs_sem,
            recv_sem=xr_sem,
            device_id=(seq, other),
            device_id_type=MESH,
        )

    lane = lax.broadcasted_iota(jnp.int32, (TOK, HEAD_SIZE), 1)
    row = lax.broadcasted_iota(jnp.int32, (TOK, HEAD_SIZE), 0)

    tab_copy.wait()
    cos_row, sin_row = tab[pl.ds(0, TOK), :], tab[pl.ds(TOK, TOK), :]
    cos_base = tab[pl.ds(2 * TOK + seq, 1), :]
    sin_base = tab[pl.ds(2 * TOK + N_SEQ + seq, 1), :]
    cosine = cos_row * cos_base - sin_row * sin_base
    sine = sin_row * cos_base + cos_row * sin_base
    sine = jnp.where(lane < HEAD_SIZE // 2, -sine, sine)
    scale = HEAD_SIZE ** (-0.5) * math.log2(math.e)
    rope[0] = cosine
    rope[1] = sine
    rope[2] = cosine * scale
    rope[3] = sine * scale

    def rotated(value, which, rows):
        turned = pltpu.roll(value, HEAD_SIZE // 2, 1)
        return (value * rope[which, rows] + turned * rope[which + 1, rows]).astype(jnp.bfloat16)

    def unit_rows(half, slot):
        core = head if half == 0 else other
        return pl.ds(pl.multiple_of(slot * TOK + core * HALF, HALF), HALF)

    def remote(half, h, source, target, device):
        return pltpu.make_async_remote_copy(
            src_ref=kv.at[:, h, unit_rows(half, source), :],
            dst_ref=kv.at[:, h, unit_rows(half, target), :],
            send_sem=kv_send.at[half * KV_HERE + h, target],
            recv_sem=kv_recv.at[half * KV_HERE + h, target],
            device_id=(device, head),
            device_id_type=MESH,
        )

    def send_own(half, h):
        @pl.when(has_later)
        def _():
            remote(half, h, 0, AT4, later).start()

        @pl.when(jnp.logical_not(last))
        def _():
            remote(half, h, 0, AT1, right).start()

        @pl.when(first)
        def _():
            remote(half, h, 0, AT3, left).start()

        @pl.when(low)
        def _():
            remote(half, h, 0, AT2, far).start()

    def pass_on(half, h):
        @pl.when(has_earlier)
        def _():
            remote(half, h, 0, AT4, later).wait_recv()

        @pl.when(jnp.logical_not(first))
        def _():
            remote(half, h, 4, AT3, left).start()

        @pl.when(last)
        def _():
            remote(half, h, 4, AT1, right).start()

        @pl.when(jnp.logical_not(low))
        def _():
            remote(half, h, 4, AT2, far).start()

    def project_kv(half, h):
        rows = own_rows if half == 0 else other_rows
        both = jnp.dot(x[rows, :], wkv[h], preferred_element_type=jnp.float32)
        kv[0, h, unit_rows(half, 0), :] = rotated(both[:, :HEAD_SIZE], 0, rows)
        kv[1, h, unit_rows(half, 0), :] = both[:, HEAD_SIZE:].astype(jnp.bfloat16)

    def project_own(h, carry):
        for copy in wkv_copies(h):
            copy.wait()
        wq_copy(h).start()
        project_kv(0, h)
        return carry

    x_copy.wait()
    lax.fori_loop(0, 2, project_own, 0)

    callers = 4 + has_later.astype(jnp.int32) + has_earlier.astype(jnp.int32)
    pl.semaphore_wait(barrier, callers)
    x_exchange().start()
    send_own(0, 0)
    send_own(0, 1)
    lax.fori_loop(2, KV_HERE, project_own, 0)

    base = seq * TOK
    position = base + lax.broadcasted_iota(jnp.int32, (8, TOK), 1)

    def next_doc(number, state):
        end, start = state
        end = end + docs[number]
        return end, jnp.where(end <= position, end, start)

    _, start_row = lax.fori_loop(
        0, DOCS, next_doc, (jnp.int32(0), jnp.zeros((8, TOK), jnp.int32))
    )
    start_row = start_row.astype(jnp.float32)
    start = jnp.transpose(jnp.concatenate([start_row] * (HEAD_SIZE // 8), axis=0))
    base_f = base.astype(jnp.float32)
    for slot in range(SLOTS):
        for half in range(TOK // HEAD_SIZE):
            offset = lane + half * HEAD_SIZE
            allowed = offset.astype(jnp.float32) + (base_f - float(slot * TOK)) >= start
            if slot == 0:
                allowed = allowed & (offset <= row)
            bias[:, pl.ds(slot * TOK + half * HEAD_SIZE, HEAD_SIZE)] = jnp.where(
                allowed, 0.0, NEG_FILL
            )

    @pl.when(jnp.logical_not(has_earlier))
    def _():
        kv[:, :, pl.ds(4 * TOK, TOK), :] = jnp.zeros((2, KV_HERE, TOK, HEAD_SIZE), jnp.bfloat16)

    acc[...] = jnp.zeros_like(acc)
    x_exchange().wait()

    def project_other(h, carry):
        @pl.when(h >= 2)
        def _():
            send_own(0, h)

        project_kv(1, h)
        send_own(1, h)
        return carry

    lax.fori_loop(0, KV_HERE, project_other, 0)
    pass_on(0, 0)

    def project_q(h, carry):
        wq_copy(h).wait()
        wo_copy(h).start()
        some = jnp.dot(x[...], wq[h], preferred_element_type=jnp.float32)
        for number in range(GROUP):
            q[h * GROUP + number] = rotated(
                some[:, number * HEAD_SIZE : (number + 1) * HEAD_SIZE], 2, slice(None)
            )
        for step, (half, head_number) in enumerate(((0, 1), (1, 0), (1, 1), (0, 2))):
            @pl.when(h == step)
            def _():
                pass_on(half, head_number)

        return carry

    lax.fori_loop(0, KV_HERE, project_q, 0)
    pass_on(1, 2)

    def reduce_copy(chunk):
        return pltpu.make_async_remote_copy(
            src_ref=send.at[chunk],
            dst_ref=recv.at[chunk],
            send_sem=red_send.at[chunk],
            recv_sem=red_recv.at[chunk],
            device_id=(seq, other),
            device_id_type=MESH,
        )

    def attend(h, carry):
        for half in range(2):
            for slot in (AT1, AT2, AT3):
                remote(half, h, 0, slot, far).wait_recv()
        keys = kv[0, h, pl.ds(0, SLOTS * TOK), :]
        values = kv[1, h, pl.ds(0, SLOTS * TOK), :]
        values = jnp.concatenate([values, jnp.ones_like(values)], axis=1)
        for number in range(GROUP):
            score = lax.dot_general(
                q[h * GROUP + number], keys, (((1,), (1,)), ((), ())),
                preferred_element_type=jnp.float32,
            )
            score = score + bias[...]
            rowmax = jnp.max(score, axis=1, keepdims=True)
            weight = jnp.exp2(score - rowmax).astype(jnp.bfloat16)
            mixed = jnp.dot(weight, values, preferred_element_type=jnp.float32)
            att[:, number * HEAD_SIZE : (number + 1) * HEAD_SIZE] = (
                mixed[:, :HEAD_SIZE] / mixed[:, HEAD_SIZE:]
            ).astype(jnp.bfloat16)

        @pl.when(h == 0)
        def _():
            pass_on(0, 3)
            pass_on(1, 3)

        wo_copy(h).wait()

        def project_out(chunk, inner):
            columns = lanes(chunk, WIDE_COLS)
            acc[:, columns] += jnp.dot(
                att[...], wo[h, :, columns], preferred_element_type=jnp.float32
            )
            return inner

        @pl.when(h < KV_HERE - 1)
        def _():
            lax.fori_loop(0, WIDTH // WIDE_COLS, project_out, 0)

        return carry

    lax.fori_loop(0, KV_HERE, attend, 0)

    def project_last(chunk, carry):
        columns = lanes(chunk, COLS)
        acc[:, columns] += jnp.dot(
            att[...], wo[KV_HERE - 1, :, columns], preferred_element_type=jnp.float32
        )
        send[chunk] = acc[other_rows, columns].astype(jnp.bfloat16)
        reduce_copy(chunk).start()
        return carry

    lax.fori_loop(0, CHUNKS, project_last, 0)

    def finish(chunk, carry):
        columns = lanes(chunk, COLS)
        reduce_copy(chunk).wait()
        out[:, columns] = (
            acc[own_rows, columns] + recv[chunk].astype(jnp.float32)
        ).astype(jnp.bfloat16)
        return carry

    lax.fori_loop(0, CHUNKS, finish, 0)

    def sent(h, carry):
        for half in range(2):
            @pl.when(has_later)
            def _():
                remote(half, h, 0, AT4, later).wait_send()

            for slot in (AT1, AT2, AT3):
                remote(half, h, 0, slot, far).wait_send()

        return carry

    lax.fori_loop(0, KV_HERE, sent, 0)


def body(input_rows, doc_lengths, w_query, key_weight, value_weight, w_out):
    table = jnp.asarray(rotary_tables())
    hbm = pl.BlockSpec(memory_space=pl.ANY)
    dma = pltpu.SemaphoreType.DMA
    wide = GROUP * HEAD_SIZE
    return pl.pallas_call(
        kernel,
        out_shape=jax.ShapeDtypeStruct((HALF, WIDTH), jnp.bfloat16),
        in_specs=[hbm, pl.BlockSpec(memory_space=pltpu.SMEM), hbm, hbm, hbm, hbm, hbm],
        out_specs=pl.BlockSpec(memory_space=pltpu.VMEM),
        scratch_shapes=[
            pltpu.VMEM((TOK, WIDTH), jnp.bfloat16),
            pltpu.VMEM((KV_HERE, WIDTH, 2 * HEAD_SIZE), jnp.bfloat16),
            pltpu.VMEM((KV_HERE, WIDTH, wide), jnp.bfloat16),
            pltpu.VMEM((KV_HERE, wide, WIDTH), jnp.bfloat16),
            pltpu.VMEM((KV_HERE * GROUP, TOK, HEAD_SIZE), jnp.bfloat16),
            pltpu.VMEM((2, KV_HERE, SLOTS * TOK, HEAD_SIZE), jnp.bfloat16),
            pltpu.VMEM((TOK, WIDTH), jnp.float32),
            pltpu.VMEM((CHUNKS, HALF, COLS), jnp.bfloat16),
            pltpu.VMEM((CHUNKS, HALF, COLS), jnp.bfloat16),
            pltpu.VMEM((TOK, wide), jnp.bfloat16),
            pltpu.VMEM((TOK, SLOTS * TOK), jnp.float32),
            pltpu.VMEM((2 * TOK + 2 * N_SEQ, HEAD_SIZE), jnp.float32),
            pltpu.VMEM((4, TOK, HEAD_SIZE), jnp.float32),
            dma(()), dma((KV_HERE, 2)), dma((KV_HERE,)), dma((KV_HERE,)), dma(()),
            dma(()), dma(()), dma((UNITS, SLOTS)), dma((UNITS, SLOTS)), dma((CHUNKS,)), dma((CHUNKS,)),
        ],
        compiler_params=pltpu.CompilerParams(
            collective_id=0, has_side_effects=True, vmem_limit_bytes=62 << 20
        ),
        name="layer",
    )(input_rows, doc_lengths, w_query, key_weight, value_weight, w_out, table)


def solution(mesh):
    in_specs = (
        P(("seq", "head"), None),
        P(),
        P(None, "head"),
        P(None, "head"),
        P(None, "head"),
        P("head", None),
    )
    out_specs = P(("seq", "head"), None)
    return jax.shard_map(body, mesh=mesh, in_specs=in_specs, out_specs=out_specs, check_vma=False)
```

```python
import math

import jax
import jax.numpy as jnp
import numpy as np
from jax import lax
from jax.experimental import pallas as pl
from jax.experimental.pallas import tpu as pltpu
from jax.sharding import PartitionSpec as P

MESH = pl.DeviceIdType.MESH
HEAD_SIZE = 128
TOK = 256
HALF = 128
WIDTH = 4096
KV_HERE = 4
GROUP = 4
SLOTS = 5
X_RING = 4
N_SEQ = 128
DOCS = 64
NEG_FILL = -1e30
COLS = 1024
CHUNKS = WIDTH // COLS
TILE = GROUP * HEAD_SIZE
PLACES = 6
WIDE_COLS = 2048

UNITS = 2 * KV_HERE
ORDER = ((0, 0), (0, 1), (1, 0), (1, 1), (0, 2), (1, 2), (0, 3), (1, 3))
KEY, VALUE, BOTH = 0, 1, slice(None)
PLACE_OF = (0, 1, 4, 2, 3)
EARLY = 4 * TOK
AT4, AT1, AT3, AT2K, AT2V = range(5)
TO4, TO1, TO3, STRAIGHT, ON_RIGHT, ON_LEFT = range(6)


def inverse_frequency():
    table = []
    for number in range(HEAD_SIZE // 2):
        base_freq = 500000.0 ** (-(2.0 * number) / HEAD_SIZE)
        wavelength = 2.0 * math.pi / base_freq
        smooth = (8192.0 / wavelength - 1.0) / 3.0
        if wavelength < 2048.0:
            table.append(base_freq)
        elif wavelength > 8192.0:
            table.append(base_freq / 8.0)
        else:
            table.append((1.0 - smooth) * base_freq / 8.0 + smooth * base_freq)
    return np.asarray(table, dtype=np.float32).astype(np.float64)


def rotary_tables():
    freq = np.concatenate([inverse_frequency()] * 2)
    rows = np.arange(TOK)[:, None] * freq
    starts = (np.arange(N_SEQ) * TOK)[:, None] * freq
    return np.concatenate(
        [np.cos(rows), np.sin(rows), np.cos(starts), np.sin(starts)]
    ).astype(np.float32)


def kernel(
    x_hbm, docs, wq_hbm, wk_hbm, wv_hbm, wo_hbm, tab_hbm,
    out,
    x, wkv, weights, q, kv, acc, send, recv, att, bias, tab, rope, partial, top,
    x_sem, wkv_sem, wq_sem, wo_sem, tab_sem,
    xs_sem, xr_sem, kv_send, kv_recv, red_send, red_recv,
):
    seq = lax.axis_index("seq")
    head = lax.axis_index("head")
    other = 1 - head
    place = lax.rem(seq, X_RING)
    right = jnp.where(place == X_RING - 1, seq - (X_RING - 1), seq + 1)
    left = jnp.where(place == 0, seq + (X_RING - 1), seq - 1)
    first = place == 0
    last = place == X_RING - 1
    low = place < X_RING // 2
    far = jnp.where(low, seq + 2, seq - 2)
    has_later = seq < N_SEQ - X_RING
    has_earlier = seq >= X_RING
    later = jnp.where(has_later, seq + X_RING, seq)
    earlier = jnp.where(has_earlier, seq - X_RING, seq)
    own_rows = pl.ds(pl.multiple_of(head * HALF, HALF), HALF)
    other_rows = pl.ds(pl.multiple_of(other * HALF, HALF), HALF)

    x_copy = pltpu.make_async_copy(x_hbm, x.at[own_rows, :], x_sem)
    tab_copy = pltpu.make_async_copy(tab_hbm, tab, tab_sem)

    def lanes(number, size):
        return pl.ds(pl.multiple_of(number * size, size), size)

    def wkv_copies(h):
        return (
            pltpu.make_async_copy(
                wk_hbm.at[:, lanes(h, HEAD_SIZE)], wkv.at[h, :, pl.ds(0, HEAD_SIZE)], wkv_sem.at[h, 0]
            ),
            pltpu.make_async_copy(
                wv_hbm.at[:, lanes(h, HEAD_SIZE)],
                wkv.at[h, :, pl.ds(HEAD_SIZE, HEAD_SIZE)],
                wkv_sem.at[h, 1],
            ),
        )

    def wq_copy(h):
        return pltpu.make_async_copy(
            wq_hbm.at[:, :, lanes(h, TILE)], weights.at[h], wq_sem.at[h]
        )

    def wo_place(h):
        return lax.rem(h + KV_HERE, PLACES)

    def wo_copies(h):
        return [
            pltpu.make_async_copy(
                wo_hbm.at[lanes(h, TILE), pl.ds(block * TILE, TILE)],
                weights.at[wo_place(h), block], wo_sem.at[h, block],
            )
            for block in range(WIDTH // TILE)
        ]

    def start_all(copies):
        for copy in copies:
            copy.start()

    def wait_all(copies):
        for copy in copies:
            copy.wait()

    def projected_out(h, first_block, blocks):
        place = wo_place(h)
        return [
            jnp.dot(att[...], weights[place, first_block + block], preferred_element_type=jnp.float32)
            for block in range(blocks)
        ]

    x_copy.start()
    tab_copy.start()
    for h in range(KV_HERE):
        for copy in wkv_copies(h):
            copy.start()

    barrier = pltpu.get_barrier_semaphore()

    def greet(target):
        pl.semaphore_signal(barrier, inc=1, device_id=target, device_id_type=MESH)

    for target in ((seq, other), (right, head), (left, head), (far, head)):
        greet(target)

    @pl.when(has_later)
    def _():
        greet((later, head))

    @pl.when(has_earlier)
    def _():
        greet((earlier, head))

    def x_exchange():
        return pltpu.make_async_remote_copy(
            src_ref=x_hbm,
            dst_ref=x.at[own_rows, :],
            send_sem=xs_sem,
            recv_sem=xr_sem,
            device_id=(seq, other),
            device_id_type=MESH,
        )

    lane = lax.broadcasted_iota(jnp.int32, (TOK, HEAD_SIZE), 1)
    row = lax.broadcasted_iota(jnp.int32, (TOK, HEAD_SIZE), 0)

    tab_copy.wait()
    cos_row, sin_row = tab[pl.ds(0, TOK), :], tab[pl.ds(TOK, TOK), :]
    cos_base = tab[pl.ds(2 * TOK + seq, 1), :]
    sin_base = tab[pl.ds(2 * TOK + N_SEQ + seq, 1), :]
    cosine = cos_row * cos_base - sin_row * sin_base
    sine = sin_row * cos_base + cos_row * sin_base
    sine = jnp.where(lane < HEAD_SIZE // 2, -sine, sine)
    scale = HEAD_SIZE ** (-0.5) * math.log2(math.e)
    rope[0] = cosine
    rope[1] = sine
    rope[2] = cosine * scale
    rope[3] = sine * scale

    def rotated(value, which, rows):
        turned = pltpu.roll(value, HEAD_SIZE // 2, 1)
        return (value * rope[which, rows] + turned * rope[which + 1, rows]).astype(jnp.bfloat16)

    def unit_rows(half, slot):
        core = head if half == 0 else other
        return pl.ds(pl.multiple_of(PLACE_OF[slot] * TOK + core * HALF, HALF), HALF)

    def remote(unit, parts, source, target, leaving, landing, device):
        half, h = unit
        return pltpu.make_async_remote_copy(
            src_ref=kv.at[parts, h, unit_rows(half, source), :],
            dst_ref=kv.at[parts, h, unit_rows(half, target), :],
            send_sem=kv_send.at[half * KV_HERE + h, leaving],
            recv_sem=kv_recv.at[half * KV_HERE + h, landing],
            device_id=(device, head),
            device_id_type=MESH,
        )

    def landed(unit, landing):
        parts = (BOTH, BOTH, BOTH, KEY, VALUE)[landing]
        slot = (4, 1, 3, 2, 2)[landing]
        remote(unit, parts, slot, slot, TO4, landing, right).wait_recv()

    def send_own(half, h):
        unit = (half, h)

        @pl.when(has_later)
        def _():
            remote(unit, BOTH, 0, 4, TO4, AT4, later).start()

        @pl.when(jnp.logical_not(last))
        def _():
            remote(unit, BOTH, 0, 1, TO1, AT1, right).start()

        @pl.when(first)
        def _():
            remote(unit, BOTH, 0, 3, TO3, AT3, left).start()

        @pl.when(place == 1)
        def _():
            remote(unit, KEY, 0, 2, STRAIGHT, AT2K, far).start()

    def pass_on(number):
        unit = ORDER[number]

        @pl.when(has_earlier)
        def _():
            landed(unit, AT4)

        @pl.when(jnp.logical_not(first))
        def _():
            remote(unit, BOTH, 4, 3, TO3, AT3, left).start()

        @pl.when(last)
        def _():
            remote(unit, BOTH, 4, 1, TO1, AT1, right).start()
            landed(unit, AT3)
            remote(unit, VALUE, 3, 2, ON_LEFT, AT2V, left).start()

        @pl.when(place == 2)
        def _():
            remote(unit, KEY, 4, 2, STRAIGHT, AT2K, far).start()

        @pl.when((place == 1) | (place == 2))
        def _():
            landed(unit, AT1)

            @pl.when(place == 1)
            def _():
                remote(unit, KEY, 1, 2, ON_RIGHT, AT2K, right).start()

            @pl.when(place == 2)
            def _():
                remote(unit, VALUE, 1, 2, ON_RIGHT, AT2V, right).start()

    def pass_far(number):
        unit = ORDER[number]

        @pl.when(first)
        def _():
            landed(unit, AT1)
            remote(unit, KEY, 1, 2, ON_RIGHT, AT2K, right).start()

        @pl.when((place == 1) | (place == 2))
        def _():
            landed(unit, AT3)
            remote(unit, VALUE, 3, 2, ON_LEFT, AT2V, left).start()

    def project_kv(half, h):
        rows = own_rows if half == 0 else other_rows
        both = jnp.dot(x[rows, :], wkv[h], preferred_element_type=jnp.float32)
        kv[0, h, unit_rows(half, 0), :] = rotated(both[:, :HEAD_SIZE], 0, rows)
        kv[1, h, unit_rows(half, 0), :] = both[:, HEAD_SIZE:].astype(jnp.bfloat16)

    def project_own(h, carry):
        for copy in wkv_copies(h):
            copy.wait()
        wq_copy(h).start()
        project_kv(0, h)
        return carry

    x_copy.wait()
    lax.fori_loop(0, 2, project_own, 0)

    callers = 4 + has_later.astype(jnp.int32) + has_earlier.astype(jnp.int32)
    pl.semaphore_wait(barrier, callers)
    x_exchange().start()
    send_own(0, 0)
    send_own(0, 1)
    lax.fori_loop(2, KV_HERE, project_own, 0)

    base = seq * TOK
    position = base + lax.broadcasted_iota(jnp.int32, (8, TOK), 1)

    def next_doc(number, state):
        end, start = state
        end = end + docs[number]
        return end, jnp.where(end <= position, end, start)

    _, start_row = lax.fori_loop(
        0, DOCS, next_doc, (jnp.int32(0), jnp.zeros((8, TOK), jnp.int32))
    )
    start_row = start_row.astype(jnp.float32)
    start = jnp.transpose(jnp.concatenate([start_row] * (HEAD_SIZE // 8), axis=0))
    base_f = base.astype(jnp.float32)
    for slot in range(SLOTS):
        for half in range(TOK // HEAD_SIZE):
            offset = lane + half * HEAD_SIZE
            allowed = offset.astype(jnp.float32) + (base_f - float(slot * TOK)) >= start
            if slot == 0:
                allowed = allowed & (offset <= row)
            bias[:, pl.ds(PLACE_OF[slot] * TOK + half * HEAD_SIZE, HEAD_SIZE)] = jnp.where(
                allowed, 0.0, NEG_FILL
            )

    @pl.when(jnp.logical_not(has_earlier))
    def _():
        kv[:, :, pl.ds(PLACE_OF[4] * TOK, TOK), :] = jnp.zeros((2, KV_HERE, TOK, HEAD_SIZE), jnp.bfloat16)

    acc[...] = jnp.zeros_like(acc)
    x_exchange().wait()

    def project_other(h, carry):
        @pl.when(h >= 2)
        def _():
            send_own(0, h)

        project_kv(1, h)
        send_own(1, h)
        return carry

    lax.fori_loop(0, KV_HERE, project_other, 0)
    pass_on(0)
    after_query = (
        lambda: pass_on(1),
        lambda: pass_on(2),
        lambda: (pass_on(3), pass_far(0)),
        lambda: (pass_on(4), pass_far(1)),
    )

    def project_q(h, carry):
        @pl.when(h < PLACES - KV_HERE)
        def _():
            start_all(wo_copies(h))

        wq_copy(h).wait()
        columns = weights[h].reshape(WIDTH, TILE)
        some = jnp.dot(x[...], columns, preferred_element_type=jnp.float32)
        for number in range(GROUP):
            q[h * GROUP + number] = rotated(
                some[:, number * HEAD_SIZE : (number + 1) * HEAD_SIZE], 2, slice(None)
            )

        @pl.when(h < 2 * KV_HERE - PLACES)
        def _():
            start_all(wo_copies(h + PLACES - KV_HERE))

        for step, actions in enumerate(after_query):
            @pl.when(h == step)
            def _():
                actions()

        return carry

    lax.fori_loop(0, KV_HERE, project_q, 0)
    def reduce_copy(chunk):
        return pltpu.make_async_remote_copy(
            src_ref=send.at[chunk],
            dst_ref=recv.at[chunk],
            send_sem=red_send.at[chunk],
            recv_sem=red_recv.at[chunk],
            device_id=(seq, other),
            device_id_type=MESH,
        )

    def values_of(h, rows):
        values = kv[VALUE, h, rows, :]
        return jnp.concatenate([values, jnp.ones_like(values)], axis=1)

    def scores_of(h, number, rows):
        score = lax.dot_general(
            q[h * GROUP + number], kv[KEY, h, rows, :], (((1,), (1,)), ((), ())),
            preferred_element_type=jnp.float32,
        )
        return score + bias[:, rows]

    def attend_early(h):
        for half in range(2):
            @pl.when(last)
            def _():
                landed((half, h), AT1)

            @pl.when(first)
            def _():
                landed((half, h), AT3)

        rows = slice(0, EARLY)
        values = values_of(h, rows)
        for number in range(GROUP):
            score = scores_of(h, number, rows)
            rowmax = jnp.max(score, axis=1, keepdims=True)
            weight = jnp.exp2(score - rowmax).astype(jnp.bfloat16)
            kept = lax.rem(h, 2) * GROUP + number
            partial[kept] = jnp.dot(weight, values, preferred_element_type=jnp.float32)
            top[kept] = jnp.broadcast_to(rowmax, (TOK, HEAD_SIZE))

    def attend_late(h):
        for half in range(2):
            landed((half, h), AT2K)
            landed((half, h), AT2V)

        rows = slice(EARLY, SLOTS * TOK)
        values = values_of(h, rows)
        for number in range(GROUP):
            kept = lax.rem(h, 2) * GROUP + number
            score = scores_of(h, number, rows)
            before = top[kept]
            rowmax = jnp.maximum(before, jnp.max(score, axis=1, keepdims=True))
            factor = jnp.exp2(before - rowmax)
            weight = jnp.exp2(score - jnp.concatenate([rowmax, rowmax], axis=1))
            mixed = jnp.dot(weight.astype(jnp.bfloat16), values, preferred_element_type=jnp.float32)
            mixed = mixed + partial[kept] * jnp.concatenate([factor, factor], axis=1)
            att[:, number * HEAD_SIZE : (number + 1) * HEAD_SIZE] = (
                mixed[:, :HEAD_SIZE] / mixed[:, HEAD_SIZE:]
            ).astype(jnp.bfloat16)

    def project_out(h):
        wait_all(wo_copies(h))

        def some(chunk, carry):
            blocks = WIDE_COLS // TILE
            for block, sums in enumerate(projected_out(h, chunk * blocks, blocks)):
                acc[:, lanes(chunk * blocks + block, TILE)] += sums
            return carry

        lax.fori_loop(0, WIDTH // WIDE_COLS, some, 0)

    def attend(step, carry):
        def at(number, *actions):
            @pl.when(step == number)
            def _():
                for action, unit in actions:
                    action(unit)

        at(0, (pass_on, 5), (pass_far, 2))
        at(1, (pass_on, 6), (pass_far, 3))
        at(2, (pass_far, 5))

        @pl.when(step < KV_HERE)
        def _():
            attend_early(step)

        at(1, (pass_on, 7), (pass_far, 4))
        at(2, (pass_far, 6))

        @pl.when(step >= 1)
        def _():
            attend_late(step - 1)

        at(2, (pass_far, 7))

        @pl.when((step >= 1) & (step < KV_HERE))
        def _():
            project_out(step - 1)

        return carry

    lax.fori_loop(0, KV_HERE + 1, attend, 0)
    wait_all(wo_copies(KV_HERE - 1))

    def project_last(chunk, carry):
        columns = lanes(chunk, COLS)
        blocks = COLS // TILE
        for block, sums in enumerate(projected_out(KV_HERE - 1, chunk * blocks, blocks)):
            acc[:, lanes(chunk * blocks + block, TILE)] += sums
        send[chunk] = acc[other_rows, columns].astype(jnp.bfloat16)
        reduce_copy(chunk).start()
        return carry

    lax.fori_loop(0, CHUNKS, project_last, 0)

    def finish(chunk, carry):
        columns = lanes(chunk, COLS)
        reduce_copy(chunk).wait()
        out[:, columns] = (
            acc[own_rows, columns] + recv[chunk].astype(jnp.float32)
        ).astype(jnp.bfloat16)
        return carry

    lax.fori_loop(0, CHUNKS, finish, 0)

    def sent(h, carry):
        for half in range(2):
            def gone(parts, leaving):
                remote((half, h), parts, 0, 0, leaving, AT4, right).wait_send()

            gone(BOTH, TO1)
            gone(BOTH, TO3)

            @pl.when(has_later)
            def _():
                gone(BOTH, TO4)

            @pl.when((place == 1) | (place == 2))
            def _():
                gone(KEY, STRAIGHT)

            @pl.when(jnp.logical_not(last))
            def _():
                gone(KEY, ON_RIGHT)

            @pl.when(jnp.logical_not(first))
            def _():
                gone(VALUE, ON_LEFT)

        return carry

    lax.fori_loop(0, KV_HERE, sent, 0)


def body(input_rows, doc_lengths, w_query, key_weight, value_weight, w_out):
    table = jnp.asarray(rotary_tables())
    hbm = pl.BlockSpec(memory_space=pl.ANY)
    dma = pltpu.SemaphoreType.DMA
    wide = GROUP * HEAD_SIZE
    return pl.pallas_call(
        kernel,
        out_shape=jax.ShapeDtypeStruct((HALF, WIDTH), jnp.bfloat16),
        in_specs=[hbm, pl.BlockSpec(memory_space=pltpu.SMEM), hbm, hbm, hbm, hbm, hbm],
        out_specs=pl.BlockSpec(memory_space=pltpu.VMEM),
        scratch_shapes=[
            pltpu.VMEM((TOK, WIDTH), jnp.bfloat16),
            pltpu.VMEM((KV_HERE, WIDTH, 2 * HEAD_SIZE), jnp.bfloat16),
            pltpu.VMEM((PLACES, WIDTH // TILE, TILE, TILE), jnp.bfloat16),
            pltpu.VMEM((KV_HERE * GROUP, TOK, HEAD_SIZE), jnp.bfloat16),
            pltpu.VMEM((2, KV_HERE, SLOTS * TOK, HEAD_SIZE), jnp.bfloat16),
            pltpu.VMEM((TOK, WIDTH), jnp.float32),
            pltpu.VMEM((CHUNKS, HALF, COLS), jnp.bfloat16),
            pltpu.VMEM((CHUNKS, HALF, COLS), jnp.bfloat16),
            pltpu.VMEM((TOK, wide), jnp.bfloat16),
            pltpu.VMEM((TOK, SLOTS * TOK), jnp.float32),
            pltpu.VMEM((2 * TOK + 2 * N_SEQ, HEAD_SIZE), jnp.float32),
            pltpu.VMEM((4, TOK, HEAD_SIZE), jnp.float32),
            pltpu.VMEM((2 * GROUP, TOK, 2 * HEAD_SIZE), jnp.float32),
            pltpu.VMEM((2 * GROUP, TOK, HEAD_SIZE), jnp.float32),
            dma(()), dma((KV_HERE, 2)), dma((KV_HERE,)), dma((KV_HERE, WIDTH // TILE)), dma(()),
            dma(()), dma(()), dma((UNITS, 6)), dma((UNITS, 5)), dma((CHUNKS,)), dma((CHUNKS,)),
        ],
        compiler_params=pltpu.CompilerParams(
            collective_id=0, has_side_effects=True, vmem_limit_bytes=52 << 20
        ),
        name="layer",
    )(input_rows, doc_lengths, w_query.reshape(WIDTH // TILE, TILE, -1), key_weight, value_weight, w_out, table)


def solution(mesh):
    in_specs = (
        P(("seq", "head"), None),
        P(),
        P(None, "head"),
        P(None, "head"),
        P(None, "head"),
        P("head", None),
    )
    out_specs = P(("seq", "head"), None)
    return jax.shard_map(body, mesh=mesh, in_specs=in_specs, out_specs=out_specs, check_vma=False)
```

```python
import math

import jax
import jax.numpy as jnp
import numpy as np
from jax import lax
from jax.experimental import pallas as pl
from jax.experimental.pallas import tpu as pltpu
from jax.sharding import PartitionSpec as P

MESH = pl.DeviceIdType.MESH
HEAD_SIZE = 128
TOK = 256
HALF = 128
WIDTH = 4096
KV_HERE = 4
GROUP = 4
SLOTS = 5
X_RING = 4
N_SEQ = 128
DOCS = 64
NEG_FILL = -1e30
COLS = 1024
CHUNKS = WIDTH // COLS
TILE = GROUP * HEAD_SIZE
PLACES = 6
WIDE_COLS = 2048

UNITS = 2 * KV_HERE
ORDER = ((0, 0), (0, 1), (1, 0), (1, 1), (0, 2), (1, 2), (0, 3), (1, 3))
KEY, VALUE, BOTH = 0, 1, slice(None)
PLACE_OF = (0, 1, 4, 2, 3)
EARLY = 4 * TOK
AT4, AT1, AT3, AT2K, AT2V = range(5)
TO4, TO1, TO3, STRAIGHT, ON_RIGHT, ON_LEFT = range(6)


def inverse_frequency():
    table = []
    for number in range(HEAD_SIZE // 2):
        base_freq = 500000.0 ** (-(2.0 * number) / HEAD_SIZE)
        wavelength = 2.0 * math.pi / base_freq
        smooth = (8192.0 / wavelength - 1.0) / 3.0
        if wavelength < 2048.0:
            table.append(base_freq)
        elif wavelength > 8192.0:
            table.append(base_freq / 8.0)
        else:
            table.append((1.0 - smooth) * base_freq / 8.0 + smooth * base_freq)
    return np.asarray(table, dtype=np.float32).astype(np.float64)


SUBLANES = 8
SCORE_SCALE = HEAD_SIZE ** (-0.5) * math.log2(math.e)


def rotary_tables():
    freq = np.concatenate([inverse_frequency()] * 2)
    rows = np.arange(TOK)[:, None] * freq
    starts = np.repeat(np.arange(N_SEQ) * TOK, SUBLANES)[:, None] * freq
    offsets = [np.cos(rows), np.sin(rows)]
    scaled = [SCORE_SCALE * table for table in offsets]
    return np.concatenate(offsets + scaled + [np.cos(starts), np.sin(starts)]).astype(np.float32)


def kernel(
    x_hbm, docs, wq_hbm, wk_hbm, wv_hbm, wo_hbm, tab_hbm,
    out,
    x, wkv, weights, q, kv, acc, send, recv, att, bias, tab, rope, partial, top,
    x_sem, wkv_sem, wq_sem, wo_sem, tab_sem,
    xs_sem, xr_sem, kv_send, kv_recv, red_send, red_recv,
):
    seq = lax.axis_index("seq")
    head = lax.axis_index("head")
    other = 1 - head
    place = lax.rem(seq, X_RING)
    right = jnp.where(place == X_RING - 1, seq - (X_RING - 1), seq + 1)
    left = jnp.where(place == 0, seq + (X_RING - 1), seq - 1)
    first = place == 0
    last = place == X_RING - 1
    low = place < X_RING // 2
    far = jnp.where(low, seq + 2, seq - 2)
    has_later = seq < N_SEQ - X_RING
    has_earlier = seq >= X_RING
    later = jnp.where(has_later, seq + X_RING, seq)
    earlier = jnp.where(has_earlier, seq - X_RING, seq)
    own_rows = pl.ds(pl.multiple_of(head * HALF, HALF), HALF)
    other_rows = pl.ds(pl.multiple_of(other * HALF, HALF), HALF)

    x_copy = pltpu.make_async_copy(x_hbm, x.at[own_rows, :], x_sem)
    starts_at = 4 * TOK
    tab_copies = [
        pltpu.make_async_copy(
            tab_hbm.at[pl.ds(pl.multiple_of(source, SUBLANES), rows), :], tab.at[pl.ds(target, rows), :], tab_sem.at[number]
        )
        for number, (source, target, rows) in enumerate(
            (
                (0, 0, starts_at),
                (starts_at + seq * SUBLANES, starts_at, SUBLANES),
                (starts_at + (N_SEQ + seq) * SUBLANES, starts_at + SUBLANES, SUBLANES),
            )
        )
    ]

    def lanes(number, size):
        return pl.ds(pl.multiple_of(number * size, size), size)

    def wkv_copies(h):
        return (
            pltpu.make_async_copy(
                wk_hbm.at[:, lanes(h, HEAD_SIZE)], wkv.at[h, :, pl.ds(0, HEAD_SIZE)], wkv_sem.at[h, 0]
            ),
            pltpu.make_async_copy(
                wv_hbm.at[:, lanes(h, HEAD_SIZE)],
                wkv.at[h, :, pl.ds(HEAD_SIZE, HEAD_SIZE)],
                wkv_sem.at[h, 1],
            ),
        )

    def wq_copy(h):
        return pltpu.make_async_copy(
            wq_hbm.at[:, :, lanes(h, TILE)], weights.at[h], wq_sem.at[h]
        )

    def wo_place(h):
        return lax.rem(h + KV_HERE, PLACES)

    def wo_copies(h):
        return [
            pltpu.make_async_copy(
                wo_hbm.at[lanes(h, TILE), pl.ds(block * TILE, TILE)],
                weights.at[wo_place(h), block], wo_sem.at[h, block],
            )
            for block in range(WIDTH // TILE)
        ]

    def start_all(copies):
        for copy in copies:
            copy.start()

    def wait_all(copies):
        for copy in copies:
            copy.wait()

    def projected_out(h, first_block, blocks):
        place = wo_place(h)
        return [
            jnp.dot(att[...], weights[place, first_block + block], preferred_element_type=jnp.float32)
            for block in range(blocks)
        ]

    x_copy.start()
    for copy in tab_copies:
        copy.start()
    for h in range(KV_HERE):
        for copy in wkv_copies(h):
            copy.start()

    barrier = pltpu.get_barrier_semaphore()

    def greet(target):
        pl.semaphore_signal(barrier, inc=1, device_id=target, device_id_type=MESH)

    for target in ((seq, other), (right, head), (left, head), (far, head)):
        greet(target)

    @pl.when(has_later)
    def _():
        greet((later, head))

    @pl.when(has_earlier)
    def _():
        greet((earlier, head))

    def x_exchange():
        return pltpu.make_async_remote_copy(
            src_ref=x_hbm,
            dst_ref=x.at[own_rows, :],
            send_sem=xs_sem,
            recv_sem=xr_sem,
            device_id=(seq, other),
            device_id_type=MESH,
        )

    lane = lax.broadcasted_iota(jnp.int32, (TOK, HEAD_SIZE), 1)
    row = lax.broadcasted_iota(jnp.int32, (TOK, HEAD_SIZE), 0)

    for copy in tab_copies:
        copy.wait()
    cos_base = tab[pl.ds(starts_at, 1), :]
    sin_base = tab[pl.ds(starts_at + SUBLANES, 1), :]
    for which in (0, 2):
        cos_row, sin_row = tab[pl.ds(which * TOK, TOK), :], tab[pl.ds((which + 1) * TOK, TOK), :]
        sine = sin_row * cos_base + cos_row * sin_base
        rope[which] = cos_row * cos_base - sin_row * sin_base
        rope[which + 1] = jnp.where(lane < HEAD_SIZE // 2, -sine, sine)

    def rotated(value, which, rows):
        turned = pltpu.roll(value, HEAD_SIZE // 2, 1)
        return (value * rope[which, rows] + turned * rope[which + 1, rows]).astype(jnp.bfloat16)

    def unit_rows(half, slot):
        core = head if half == 0 else other
        return pl.ds(pl.multiple_of(PLACE_OF[slot] * TOK + core * HALF, HALF), HALF)

    def remote(unit, parts, source, target, leaving, landing, device):
        half, h = unit
        return pltpu.make_async_remote_copy(
            src_ref=kv.at[parts, h, unit_rows(half, source), :],
            dst_ref=kv.at[parts, h, unit_rows(half, target), :],
            send_sem=kv_send.at[half * KV_HERE + h, leaving],
            recv_sem=kv_recv.at[half * KV_HERE + h, landing],
            device_id=(device, head),
            device_id_type=MESH,
        )

    def landed(unit, landing):
        parts = (BOTH, BOTH, BOTH, KEY, VALUE)[landing]
        slot = (4, 1, 3, 2, 2)[landing]
        remote(unit, parts, slot, slot, TO4, landing, right).wait_recv()

    def send_own(half, h):
        unit = (half, h)

        @pl.when(has_later)
        def _():
            remote(unit, BOTH, 0, 4, TO4, AT4, later).start()

        @pl.when(jnp.logical_not(last))
        def _():
            remote(unit, BOTH, 0, 1, TO1, AT1, right).start()

        @pl.when(first)
        def _():
            remote(unit, BOTH, 0, 3, TO3, AT3, left).start()

        @pl.when(place == 1)
        def _():
            remote(unit, KEY, 0, 2, STRAIGHT, AT2K, far).start()

    def pass_on(number):
        unit = ORDER[number]

        @pl.when(has_earlier)
        def _():
            landed(unit, AT4)

        @pl.when(jnp.logical_not(first))
        def _():
            remote(unit, BOTH, 4, 3, TO3, AT3, left).start()

        @pl.when(last)
        def _():
            remote(unit, BOTH, 4, 1, TO1, AT1, right).start()

        @pl.when(place == 2)
        def _():
            remote(unit, KEY, 4, 2, STRAIGHT, AT2K, far).start()

    def pass_own_row(unit):
        @pl.when(last)
        def _():
            landed(unit, AT3)
            remote(unit, VALUE, 3, 2, ON_LEFT, AT2V, left).start()

        @pl.when((place == 1) | (place == 2))
        def _():
            landed(unit, AT1)

            @pl.when(place == 1)
            def _():
                remote(unit, KEY, 1, 2, ON_RIGHT, AT2K, right).start()

            @pl.when(place == 2)
            def _():
                remote(unit, VALUE, 1, 2, ON_RIGHT, AT2V, right).start()

    def pass_far(number):
        unit = ORDER[number]

        @pl.when(first)
        def _():
            landed(unit, AT1)
            remote(unit, KEY, 1, 2, ON_RIGHT, AT2K, right).start()

        @pl.when((place == 1) | (place == 2))
        def _():
            landed(unit, AT3)
            remote(unit, VALUE, 3, 2, ON_LEFT, AT2V, left).start()

        pass_own_row(unit)

    def project_kv(half, h):
        rows = own_rows if half == 0 else other_rows
        both = jnp.dot(x[rows, :], wkv[h], preferred_element_type=jnp.float32)
        kv[0, h, unit_rows(half, 0), :] = rotated(both[:, :HEAD_SIZE], 0, rows)
        kv[1, h, unit_rows(half, 0), :] = both[:, HEAD_SIZE:].astype(jnp.bfloat16)

    def project_own(h, carry):
        for copy in wkv_copies(h):
            copy.wait()
        wq_copy(h).start()
        project_kv(0, h)
        return carry

    x_copy.wait()
    lax.fori_loop(0, 2, project_own, 0)

    callers = 4 + has_later.astype(jnp.int32) + has_earlier.astype(jnp.int32)
    pl.semaphore_wait(barrier, callers)
    x_exchange().start()
    send_own(0, 0)
    send_own(0, 1)
    lax.fori_loop(2, KV_HERE, project_own, 0)

    base = seq * TOK
    position = base + lax.broadcasted_iota(jnp.int32, (8, TOK), 1)

    def next_doc(number, state):
        end, start = state
        end = end + docs[number]
        return end, jnp.where(end <= position, end, start)

    _, start_row = lax.fori_loop(
        0, DOCS, next_doc, (jnp.int32(0), jnp.zeros((8, TOK), jnp.int32))
    )
    start_row = start_row.astype(jnp.float32)
    start = jnp.transpose(jnp.concatenate([start_row] * (HEAD_SIZE // 8), axis=0))
    base_f = base.astype(jnp.float32)
    for slot in range(SLOTS):
        for half in range(TOK // HEAD_SIZE):
            offset = lane + half * HEAD_SIZE
            allowed = offset.astype(jnp.float32) + (base_f - float(slot * TOK)) >= start
            if slot == 0:
                allowed = allowed & (offset <= row)
            bias[:, pl.ds(PLACE_OF[slot] * TOK + half * HEAD_SIZE, HEAD_SIZE)] = jnp.where(
                allowed, 0.0, NEG_FILL
            )

    @pl.when(jnp.logical_not(has_earlier))
    def _():
        kv[:, :, pl.ds(PLACE_OF[4] * TOK, TOK), :] = jnp.zeros((2, KV_HERE, TOK, HEAD_SIZE), jnp.bfloat16)

    acc[...] = jnp.zeros_like(acc)
    x_exchange().wait()

    def project_other(h, carry):
        @pl.when(h >= 2)
        def _():
            send_own(0, h)

        project_kv(1, h)
        send_own(1, h)
        return carry

    lax.fori_loop(0, KV_HERE, project_other, 0)
    pass_on(0)
    after_query = (
        lambda: pass_on(1),
        lambda: pass_on(2),
        lambda: (pass_on(3), pass_far(0)),
        lambda: (pass_on(4), pass_far(1)),
    )

    def project_q(h, carry):
        @pl.when(h < PLACES - KV_HERE)
        def _():
            start_all(wo_copies(h))

        wq_copy(h).wait()
        columns = weights[h].reshape(WIDTH, TILE)
        some = jnp.dot(x[...], columns, preferred_element_type=jnp.float32)
        for number in range(GROUP):
            q[h * GROUP + number] = rotated(
                some[:, number * HEAD_SIZE : (number + 1) * HEAD_SIZE], 2, slice(None)
            )

        @pl.when(h < 2 * KV_HERE - PLACES)
        def _():
            start_all(wo_copies(h + PLACES - KV_HERE))

        for step, actions in enumerate(after_query):
            @pl.when(h == step)
            def _():
                actions()

        return carry

    lax.fori_loop(0, KV_HERE, project_q, 0)
    def reduce_copy(chunk):
        return pltpu.make_async_remote_copy(
            src_ref=send.at[chunk],
            dst_ref=recv.at[chunk],
            send_sem=red_send.at[chunk],
            recv_sem=red_recv.at[chunk],
            device_id=(seq, other),
            device_id_type=MESH,
        )

    def values_of(h, rows):
        values = kv[VALUE, h, rows, :]
        return jnp.concatenate([values, jnp.ones_like(values)], axis=1)

    def scores_of(h, number, rows):
        score = lax.dot_general(
            q[h * GROUP + number], kv[KEY, h, rows, :], (((1,), (1,)), ((), ())),
            preferred_element_type=jnp.float32,
        )
        return score + bias[:, rows]

    def attend_early(h):
        for half in range(2):
            @pl.when(last)
            def _():
                landed((half, h), AT1)

            @pl.when(first)
            def _():
                landed((half, h), AT3)

        rows = slice(0, EARLY)
        values = values_of(h, rows)
        for number in range(GROUP):
            score = scores_of(h, number, rows)
            rowmax = jnp.max(score, axis=1, keepdims=True)
            weight = jnp.exp2(score - rowmax).astype(jnp.bfloat16)
            kept = lax.rem(h, 2) * GROUP + number
            partial[kept] = jnp.dot(weight, values, preferred_element_type=jnp.float32)
            top[kept] = jnp.broadcast_to(rowmax, (TOK, HEAD_SIZE))

    def attend_late(h):
        for half in range(2):
            landed((half, h), AT2K)
            landed((half, h), AT2V)

        rows = slice(EARLY, SLOTS * TOK)
        values = values_of(h, rows)
        for number in range(GROUP):
            kept = lax.rem(h, 2) * GROUP + number
            score = scores_of(h, number, rows)
            before = top[kept]
            rowmax = jnp.maximum(before, jnp.max(score, axis=1, keepdims=True))
            factor = jnp.exp2(before - rowmax)
            weight = jnp.exp2(score - jnp.concatenate([rowmax, rowmax], axis=1))
            mixed = jnp.dot(weight.astype(jnp.bfloat16), values, preferred_element_type=jnp.float32)
            mixed = mixed + partial[kept] * jnp.concatenate([factor, factor], axis=1)
            att[:, number * HEAD_SIZE : (number + 1) * HEAD_SIZE] = (
                mixed[:, :HEAD_SIZE] / mixed[:, HEAD_SIZE:]
            ).astype(jnp.bfloat16)

    def project_out(h):
        wait_all(wo_copies(h))

        def some(chunk, carry):
            blocks = WIDE_COLS // TILE
            for block, sums in enumerate(projected_out(h, chunk * blocks, blocks)):
                acc[:, lanes(chunk * blocks + block, TILE)] += sums
            return carry

        lax.fori_loop(0, WIDTH // WIDE_COLS, some, 0)

    def attend(step, carry):
        def at(number, *actions):
            @pl.when(step == number)
            def _():
                for action, unit in actions:
                    action(unit)

        at(0, (pass_on, 5), (pass_far, 2))
        at(1, (pass_on, 6), (pass_far, 3))
        at(2, (pass_far, 5))

        @pl.when(step < KV_HERE)
        def _():
            attend_early(step)

        at(1, (pass_on, 7), (pass_far, 4))
        at(2, (pass_far, 6))

        @pl.when(step >= 1)
        def _():
            attend_late(step - 1)

        at(2, (pass_far, 7))

        @pl.when((step >= 1) & (step < KV_HERE))
        def _():
            project_out(step - 1)

        return carry

    lax.fori_loop(0, KV_HERE + 1, attend, 0)
    wait_all(wo_copies(KV_HERE - 1))

    def project_last(chunk, carry):
        columns = lanes(chunk, COLS)
        blocks = COLS // TILE
        for block, sums in enumerate(projected_out(KV_HERE - 1, chunk * blocks, blocks)):
            acc[:, lanes(chunk * blocks + block, TILE)] += sums
        send[chunk] = acc[other_rows, columns].astype(jnp.bfloat16)
        reduce_copy(chunk).start()
        return carry

    lax.fori_loop(0, CHUNKS, project_last, 0)

    def finish(chunk, carry):
        columns = lanes(chunk, COLS)
        reduce_copy(chunk).wait()
        out[:, columns] = (
            acc[own_rows, columns] + recv[chunk].astype(jnp.float32)
        ).astype(jnp.bfloat16)
        return carry

    lax.fori_loop(0, CHUNKS, finish, 0)

    def sent(h, carry):
        for half in range(2):
            def gone(parts, leaving):
                remote((half, h), parts, 0, 0, leaving, AT4, right).wait_send()

            gone(BOTH, TO1)
            gone(BOTH, TO3)

            @pl.when(has_later)
            def _():
                gone(BOTH, TO4)

            @pl.when((place == 1) | (place == 2))
            def _():
                gone(KEY, STRAIGHT)

            @pl.when(jnp.logical_not(last))
            def _():
                gone(KEY, ON_RIGHT)

            @pl.when(jnp.logical_not(first))
            def _():
                gone(VALUE, ON_LEFT)

        return carry

    lax.fori_loop(0, KV_HERE, sent, 0)


def body(input_rows, doc_lengths, w_query, key_weight, value_weight, w_out):
    table = jnp.asarray(rotary_tables())
    hbm = pl.BlockSpec(memory_space=pl.ANY)
    dma = pltpu.SemaphoreType.DMA
    wide = GROUP * HEAD_SIZE
    return pl.pallas_call(
        kernel,
        out_shape=jax.ShapeDtypeStruct((HALF, WIDTH), jnp.bfloat16),
        in_specs=[hbm, pl.BlockSpec(memory_space=pltpu.SMEM), hbm, hbm, hbm, hbm, hbm],
        out_specs=pl.BlockSpec(memory_space=pltpu.VMEM),
        scratch_shapes=[
            pltpu.VMEM((TOK, WIDTH), jnp.bfloat16),
            pltpu.VMEM((KV_HERE, WIDTH, 2 * HEAD_SIZE), jnp.bfloat16),
            pltpu.VMEM((PLACES, WIDTH // TILE, TILE, TILE), jnp.bfloat16),
            pltpu.VMEM((KV_HERE * GROUP, TOK, HEAD_SIZE), jnp.bfloat16),
            pltpu.VMEM((2, KV_HERE, SLOTS * TOK, HEAD_SIZE), jnp.bfloat16),
            pltpu.VMEM((TOK, WIDTH), jnp.float32),
            pltpu.VMEM((CHUNKS, HALF, COLS), jnp.bfloat16),
            pltpu.VMEM((CHUNKS, HALF, COLS), jnp.bfloat16),
            pltpu.VMEM((TOK, wide), jnp.bfloat16),
            pltpu.VMEM((TOK, SLOTS * TOK), jnp.float32),
            pltpu.VMEM((4 * TOK + 2 * SUBLANES, HEAD_SIZE), jnp.float32),
            pltpu.VMEM((4, TOK, HEAD_SIZE), jnp.float32),
            pltpu.VMEM((2 * GROUP, TOK, 2 * HEAD_SIZE), jnp.float32),
            pltpu.VMEM((2 * GROUP, TOK, HEAD_SIZE), jnp.float32),
            dma(()), dma((KV_HERE, 2)), dma((KV_HERE,)), dma((KV_HERE, WIDTH // TILE)), dma((3,)),
            dma(()), dma(()), dma((UNITS, 6)), dma((UNITS, 5)), dma((CHUNKS,)), dma((CHUNKS,)),
        ],
        compiler_params=pltpu.CompilerParams(
            collective_id=0, has_side_effects=True, vmem_limit_bytes=(52 << 20) + (1 << 19)
        ),
        name="layer",
    )(input_rows, doc_lengths, w_query.reshape(WIDTH // TILE, TILE, -1), key_weight, value_weight, w_out, table)


def solution(mesh):
    in_specs = (
        P(("seq", "head"), None),
        P(),
        P(None, "head"),
        P(None, "head"),
        P(None, "head"),
        P("head", None),
    )
    out_specs = P(("seq", "head"), None)
    return jax.shard_map(body, mesh=mesh, in_specs=in_specs, out_specs=out_specs, check_vma=False)
```

```python
import math

import jax
import jax.numpy as jnp
import numpy as np
from jax import lax
from jax.experimental import pallas as pl
from jax.experimental.pallas import tpu as pltpu
from jax.sharding import PartitionSpec as P

MESH = pl.DeviceIdType.MESH
HEAD_SIZE = 128
TOK = 256
HALF = 128
WIDTH = 4096
KV_HERE = 4
GROUP = 4
SLOTS = 5
X_RING = 4
N_SEQ = 128
DOCS = 64
NEG_FILL = -1e30
COLS = 1024
CHUNKS = WIDTH // COLS
TILE = GROUP * HEAD_SIZE
PLACES = 6
WIDE_COLS = 2048

UNITS = 2 * KV_HERE
ORDER = ((0, 0), (0, 1), (1, 0), (1, 1), (0, 2), (1, 2), (0, 3), (1, 3))
KEY, VALUE, BOTH = 0, 1, slice(None)
PLACE_OF = (0, 1, 4, 2, 3)
EARLY = 4 * TOK
AT4, AT1, AT3, AT2K, AT2V = range(5)
TO4, TO1, TO3, STRAIGHT, ON_RIGHT, ON_LEFT = range(6)


def inverse_frequency():
    table = []
    for number in range(HEAD_SIZE // 2):
        base_freq = 500000.0 ** (-(2.0 * number) / HEAD_SIZE)
        wavelength = 2.0 * math.pi / base_freq
        smooth = (8192.0 / wavelength - 1.0) / 3.0
        if wavelength < 2048.0:
            table.append(base_freq)
        elif wavelength > 8192.0:
            table.append(base_freq / 8.0)
        else:
            table.append((1.0 - smooth) * base_freq / 8.0 + smooth * base_freq)
    return np.asarray(table, dtype=np.float32).astype(np.float64)


def rotary_tables():
    freq = np.concatenate([inverse_frequency()] * 2)
    rows = np.arange(TOK)[:, None] * freq
    starts = (np.arange(N_SEQ) * TOK)[:, None] * freq
    return np.concatenate(
        [np.cos(rows), np.sin(rows), np.cos(starts), np.sin(starts)]
    ).astype(np.float32)


def kernel(
    x_hbm, docs, wq_hbm, wk_hbm, wv_hbm, wo_hbm, tab_hbm,
    out,
    x, wkv, weights, q, kv, acc, send, recv, att, bias, tab, rope, partial, top,
    x_sem, wkv_sem, wq_sem, wo_sem, tab_sem,
    xs_sem, xr_sem, kv_send, kv_recv, red_send, red_recv,
):
    seq = lax.axis_index("seq")
    head = lax.axis_index("head")
    other = 1 - head
    place = lax.rem(seq, X_RING)
    right = jnp.where(place == X_RING - 1, seq - (X_RING - 1), seq + 1)
    left = jnp.where(place == 0, seq + (X_RING - 1), seq - 1)
    first = place == 0
    last = place == X_RING - 1
    low = place < X_RING // 2
    far = jnp.where(low, seq + 2, seq - 2)
    has_later = seq < N_SEQ - X_RING
    has_earlier = seq >= X_RING
    later = jnp.where(has_later, seq + X_RING, seq)
    earlier = jnp.where(has_earlier, seq - X_RING, seq)
    own_rows = pl.ds(pl.multiple_of(head * HALF, HALF), HALF)
    other_rows = pl.ds(pl.multiple_of(other * HALF, HALF), HALF)

    x_copy = pltpu.make_async_copy(x_hbm, x.at[own_rows, :], x_sem)
    tab_copy = pltpu.make_async_copy(tab_hbm, tab, tab_sem)

    def lanes(number, size):
        return pl.ds(pl.multiple_of(number * size, size), size)

    def wkv_copies(h):
        return (
            pltpu.make_async_copy(
                wk_hbm.at[:, lanes(h, HEAD_SIZE)], wkv.at[h, :, pl.ds(0, HEAD_SIZE)], wkv_sem.at[h, 0]
            ),
            pltpu.make_async_copy(
                wv_hbm.at[:, lanes(h, HEAD_SIZE)],
                wkv.at[h, :, pl.ds(HEAD_SIZE, HEAD_SIZE)],
                wkv_sem.at[h, 1],
            ),
        )

    def wq_copy(h):
        return pltpu.make_async_copy(
            wq_hbm.at[:, :, lanes(h, TILE)], weights.at[h], wq_sem.at[h]
        )

    def wo_place(h):
        return lax.rem(h + KV_HERE, PLACES)

    def wo_copies(h):
        return [
            pltpu.make_async_copy(
                wo_hbm.at[lanes(h, TILE), pl.ds(block * TILE, TILE)],
                weights.at[wo_place(h), block], wo_sem.at[h, block],
            )
            for block in range(WIDTH // TILE)
        ]

    def start_all(copies):
        for copy in copies:
            copy.start()

    def wait_all(copies):
        for copy in copies:
            copy.wait()

    def projected_out(h, first_block, blocks):
        place = wo_place(h)
        return [
            jnp.dot(att[...], weights[place, first_block + block], preferred_element_type=jnp.float32)
            for block in range(blocks)
        ]

    x_copy.start()
    tab_copy.start()
    for h in range(KV_HERE):
        for copy in wkv_copies(h):
            copy.start()

    barrier = pltpu.get_barrier_semaphore()

    def greet(target):
        pl.semaphore_signal(barrier, inc=1, device_id=target, device_id_type=MESH)

    for target in ((seq, other), (right, head), (left, head), (far, head)):
        greet(target)

    @pl.when(has_later)
    def _():
        greet((later, head))

    @pl.when(has_earlier)
    def _():
        greet((earlier, head))

    def x_exchange():
        return pltpu.make_async_remote_copy(
            src_ref=x_hbm,
            dst_ref=x.at[own_rows, :],
            send_sem=xs_sem,
            recv_sem=xr_sem,
            device_id=(seq, other),
            device_id_type=MESH,
        )

    lane = lax.broadcasted_iota(jnp.int32, (TOK, HEAD_SIZE), 1)
    row = lax.broadcasted_iota(jnp.int32, (TOK, HEAD_SIZE), 0)

    tab_copy.wait()
    cos_row, sin_row = tab[pl.ds(0, TOK), :], tab[pl.ds(TOK, TOK), :]
    cos_base = tab[pl.ds(2 * TOK + seq, 1), :]
    sin_base = tab[pl.ds(2 * TOK + N_SEQ + seq, 1), :]
    cosine = cos_row * cos_base - sin_row * sin_base
    sine = sin_row * cos_base + cos_row * sin_base
    sine = jnp.where(lane < HEAD_SIZE // 2, -sine, sine)
    scale = HEAD_SIZE ** (-0.5) * math.log2(math.e)
    rope[0] = cosine
    rope[1] = sine
    rope[2] = cosine * scale
    rope[3] = sine * scale

    def rotated(value, which, rows):
        turned = pltpu.roll(value, HEAD_SIZE // 2, 1)
        return (value * rope[which, rows] + turned * rope[which + 1, rows]).astype(jnp.bfloat16)

    def unit_rows(half, slot):
        core = head if half == 0 else other
        return pl.ds(pl.multiple_of(PLACE_OF[slot] * TOK + core * HALF, HALF), HALF)

    def remote(unit, parts, source, target, leaving, landing, device):
        half, h = unit
        return pltpu.make_async_remote_copy(
            src_ref=kv.at[parts, h, unit_rows(half, source), :],
            dst_ref=kv.at[parts, h, unit_rows(half, target), :],
            send_sem=kv_send.at[half * KV_HERE + h, leaving],
            recv_sem=kv_recv.at[half * KV_HERE + h, landing],
            device_id=(device, head),
            device_id_type=MESH,
        )

    def landed(unit, landing):
        parts = (BOTH, BOTH, BOTH, KEY, VALUE)[landing]
        slot = (4, 1, 3, 2, 2)[landing]
        remote(unit, parts, slot, slot, TO4, landing, right).wait_recv()

    def send_own(half, h):
        unit = (half, h)

        @pl.when(has_later)
        def _():
            remote(unit, BOTH, 0, 4, TO4, AT4, later).start()

        @pl.when(jnp.logical_not(last))
        def _():
            remote(unit, BOTH, 0, 1, TO1, AT1, right).start()

        @pl.when(first)
        def _():
            remote(unit, BOTH, 0, 3, TO3, AT3, left).start()

        @pl.when(place == 1)
        def _():
            remote(unit, KEY, 0, 2, STRAIGHT, AT2K, far).start()

    def pass_on(number):
        unit = ORDER[number]

        @pl.when(has_earlier)
        def _():
            landed(unit, AT4)

        @pl.when(jnp.logical_not(first))
        def _():
            remote(unit, BOTH, 4, 3, TO3, AT3, left).start()

        @pl.when(last)
        def _():
            remote(unit, BOTH, 4, 1, TO1, AT1, right).start()

        @pl.when(place == 2)
        def _():
            remote(unit, KEY, 4, 2, STRAIGHT, AT2K, far).start()

    def pass_own_row(unit):
        @pl.when(last)
        def _():
            landed(unit, AT3)
            remote(unit, VALUE, 3, 2, ON_LEFT, AT2V, left).start()

        @pl.when((place == 1) | (place == 2))
        def _():
            landed(unit, AT1)

            @pl.when(place == 1)
            def _():
                remote(unit, KEY, 1, 2, ON_RIGHT, AT2K, right).start()

            @pl.when(place == 2)
            def _():
                remote(unit, VALUE, 1, 2, ON_RIGHT, AT2V, right).start()

    def pass_far(number):
        unit = ORDER[number]

        @pl.when(first)
        def _():
            landed(unit, AT1)
            remote(unit, KEY, 1, 2, ON_RIGHT, AT2K, right).start()

        @pl.when((place == 1) | (place == 2))
        def _():
            landed(unit, AT3)
            remote(unit, VALUE, 3, 2, ON_LEFT, AT2V, left).start()

        pass_own_row(unit)

    def project_kv(half, h):
        rows = own_rows if half == 0 else other_rows
        both = jnp.dot(x[rows, :], wkv[h], preferred_element_type=jnp.float32)
        kv[0, h, unit_rows(half, 0), :] = rotated(both[:, :HEAD_SIZE], 0, rows)
        kv[1, h, unit_rows(half, 0), :] = both[:, HEAD_SIZE:].astype(jnp.bfloat16)

    def project_own(h, carry):
        for copy in wkv_copies(h):
            copy.wait()
        wq_copy(h).start()
        project_kv(0, h)
        return carry

    x_copy.wait()
    lax.fori_loop(0, 2, project_own, 0)

    callers = 4 + has_later.astype(jnp.int32) + has_earlier.astype(jnp.int32)
    pl.semaphore_wait(barrier, callers)
    x_exchange().start()
    send_own(0, 0)
    send_own(0, 1)
    lax.fori_loop(2, KV_HERE, project_own, 0)

    base = seq * TOK
    position = base + lax.broadcasted_iota(jnp.int32, (8, TOK), 1)

    def next_doc(number, state):
        end, start = state
        end = end + docs[number]
        return end, jnp.where(end <= position, end, start)

    _, start_row = lax.fori_loop(
        0, DOCS, next_doc, (jnp.int32(0), jnp.zeros((8, TOK), jnp.int32))
    )
    start_row = start_row.astype(jnp.float32)
    start = jnp.transpose(jnp.concatenate([start_row] * (HEAD_SIZE // 8), axis=0))
    base_f = base.astype(jnp.float32)
    for slot in range(SLOTS):
        for half in range(TOK // HEAD_SIZE):
            offset = lane + half * HEAD_SIZE
            allowed = offset.astype(jnp.float32) + (base_f - float(slot * TOK)) >= start
            if slot == 0:
                allowed = allowed & (offset <= row)
            bias[:, pl.ds(PLACE_OF[slot] * TOK + half * HEAD_SIZE, HEAD_SIZE)] = jnp.where(
                allowed, 0.0, NEG_FILL
            )

    @pl.when(jnp.logical_not(has_earlier))
    def _():
        kv[:, :, pl.ds(PLACE_OF[4] * TOK, TOK), :] = jnp.zeros((2, KV_HERE, TOK, HEAD_SIZE), jnp.bfloat16)

    acc[...] = jnp.zeros_like(acc)
    x_exchange().wait()

    def project_other(h, carry):
        @pl.when(h >= 2)
        def _():
            send_own(0, h)

        project_kv(1, h)
        send_own(1, h)
        return carry

    lax.fori_loop(0, KV_HERE, project_other, 0)
    pass_on(0)
    after_query = (
        lambda: pass_on(1),
        lambda: pass_on(2),
        lambda: (pass_on(3), pass_far(0)),
        lambda: (pass_on(4), pass_far(1)),
    )

    def project_q(h, carry):
        @pl.when(h < PLACES - KV_HERE)
        def _():
            start_all(wo_copies(h))

        wq_copy(h).wait()
        columns = weights[h].reshape(WIDTH, TILE)
        some = jnp.dot(x[...], columns, preferred_element_type=jnp.float32)
        for number in range(GROUP):
            q[h * GROUP + number] = rotated(
                some[:, number * HEAD_SIZE : (number + 1) * HEAD_SIZE], 2, slice(None)
            )

        @pl.when(h < 2 * KV_HERE - PLACES)
        def _():
            start_all(wo_copies(h + PLACES - KV_HERE))

        for step, actions in enumerate(after_query):
            @pl.when(h == step)
            def _():
                actions()

        return carry

    lax.fori_loop(0, KV_HERE, project_q, 0)
    def reduce_copy(chunk):
        return pltpu.make_async_remote_copy(
            src_ref=send.at[chunk],
            dst_ref=recv.at[chunk],
            send_sem=red_send.at[chunk],
            recv_sem=red_recv.at[chunk],
            device_id=(seq, other),
            device_id_type=MESH,
        )

    def values_of(h, rows):
        values = kv[VALUE, h, rows, :]
        return jnp.concatenate([values, jnp.ones_like(values)], axis=1)

    def scores_of(h, number, rows):
        score = lax.dot_general(
            q[h * GROUP + number], kv[KEY, h, rows, :], (((1,), (1,)), ((), ())),
            preferred_element_type=jnp.float32,
        )
        return score + bias[:, rows]

    def attend_early(h):
        for half in range(2):
            @pl.when(last)
            def _():
                landed((half, h), AT1)

            @pl.when(first)
            def _():
                landed((half, h), AT3)

        rows = slice(0, EARLY)
        values = values_of(h, rows)
        for number in range(GROUP):
            score = scores_of(h, number, rows)
            rowmax = jnp.max(score, axis=1, keepdims=True)
            weight = jnp.exp2(score - rowmax).astype(jnp.bfloat16)
            kept = lax.rem(h, 2) * GROUP + number
            partial[kept] = jnp.dot(weight, values, preferred_element_type=jnp.float32)
            top[kept] = jnp.broadcast_to(rowmax, (TOK, HEAD_SIZE))

    def attend_late(h):
        for half in range(2):
            landed((half, h), AT2K)
            landed((half, h), AT2V)

        rows = slice(EARLY, SLOTS * TOK)
        values = values_of(h, rows)
        for number in range(GROUP):
            kept = lax.rem(h, 2) * GROUP + number
            score = scores_of(h, number, rows)
            before = top[kept]
            rowmax = jnp.maximum(before, jnp.max(score, axis=1, keepdims=True))
            factor = jnp.exp2(before - rowmax)
            weight = jnp.exp2(score - jnp.concatenate([rowmax, rowmax], axis=1))
            mixed = jnp.dot(weight.astype(jnp.bfloat16), values, preferred_element_type=jnp.float32)
            mixed = mixed + partial[kept] * jnp.concatenate([factor, factor], axis=1)
            att[:, number * HEAD_SIZE : (number + 1) * HEAD_SIZE] = (
                mixed[:, :HEAD_SIZE] / mixed[:, HEAD_SIZE:]
            ).astype(jnp.bfloat16)

    def project_out(h):
        wait_all(wo_copies(h))

        def some(chunk, carry):
            blocks = WIDE_COLS // TILE
            for block, sums in enumerate(projected_out(h, chunk * blocks, blocks)):
                acc[:, lanes(chunk * blocks + block, TILE)] += sums
            return carry

        lax.fori_loop(0, WIDTH // WIDE_COLS, some, 0)

    def attend(step, carry):
        def at(number, *actions):
            @pl.when(step == number)
            def _():
                for action, unit in actions:
                    action(unit)

        at(0, (pass_on, 5), (pass_far, 2))
        at(1, (pass_on, 6), (pass_far, 3))
        at(2, (pass_far, 5))

        @pl.when(step < KV_HERE)
        def _():
            attend_early(step)

        at(1, (pass_on, 7), (pass_far, 4))
        at(2, (pass_far, 6))

        @pl.when(step >= 1)
        def _():
            attend_late(step - 1)

        at(2, (pass_far, 7))

        @pl.when((step >= 1) & (step < KV_HERE))
        def _():
            project_out(step - 1)

        return carry

    lax.fori_loop(0, KV_HERE + 1, attend, 0)
    wait_all(wo_copies(KV_HERE - 1))

    def project_last(chunk, carry):
        columns = lanes(chunk, COLS)
        blocks = COLS // TILE
        for block, sums in enumerate(projected_out(KV_HERE - 1, chunk * blocks, blocks)):
            acc[:, lanes(chunk * blocks + block, TILE)] += sums
        send[chunk] = acc[other_rows, columns].astype(jnp.bfloat16)
        reduce_copy(chunk).start()
        return carry

    lax.fori_loop(0, CHUNKS, project_last, 0)

    def finish(chunk, carry):
        columns = lanes(chunk, COLS)
        reduce_copy(chunk).wait()
        out[:, columns] = (
            acc[own_rows, columns] + recv[chunk].astype(jnp.float32)
        ).astype(jnp.bfloat16)
        return carry

    lax.fori_loop(0, CHUNKS, finish, 0)

    def sent(h, carry):
        for half in range(2):
            def gone(parts, leaving):
                remote((half, h), parts, 0, 0, leaving, AT4, right).wait_send()

            gone(BOTH, TO1)
            gone(BOTH, TO3)

            @pl.when(has_later)
            def _():
                gone(BOTH, TO4)

            @pl.when((place == 1) | (place == 2))
            def _():
                gone(KEY, STRAIGHT)

            @pl.when(jnp.logical_not(last))
            def _():
                gone(KEY, ON_RIGHT)

            @pl.when(jnp.logical_not(first))
            def _():
                gone(VALUE, ON_LEFT)

        return carry

    lax.fori_loop(0, KV_HERE, sent, 0)


def body(input_rows, doc_lengths, w_query, key_weight, value_weight, w_out):
    table = jnp.asarray(rotary_tables())
    hbm = pl.BlockSpec(memory_space=pl.ANY)
    dma = pltpu.SemaphoreType.DMA
    wide = GROUP * HEAD_SIZE
    return pl.pallas_call(
        kernel,
        out_shape=jax.ShapeDtypeStruct((HALF, WIDTH), jnp.bfloat16),
        in_specs=[hbm, pl.BlockSpec(memory_space=pltpu.SMEM), hbm, hbm, hbm, hbm, hbm],
        out_specs=pl.BlockSpec(memory_space=pltpu.VMEM),
        scratch_shapes=[
            pltpu.VMEM((TOK, WIDTH), jnp.bfloat16),
            pltpu.VMEM((KV_HERE, WIDTH, 2 * HEAD_SIZE), jnp.bfloat16),
            pltpu.VMEM((PLACES, WIDTH // TILE, TILE, TILE), jnp.bfloat16),
            pltpu.VMEM((KV_HERE * GROUP, TOK, HEAD_SIZE), jnp.bfloat16),
            pltpu.VMEM((2, KV_HERE, SLOTS * TOK, HEAD_SIZE), jnp.bfloat16),
            pltpu.VMEM((TOK, WIDTH), jnp.float32),
            pltpu.VMEM((CHUNKS, HALF, COLS), jnp.bfloat16),
            pltpu.VMEM((CHUNKS, HALF, COLS), jnp.bfloat16),
            pltpu.VMEM((TOK, wide), jnp.bfloat16),
            pltpu.VMEM((TOK, SLOTS * TOK), jnp.float32),
            pltpu.VMEM((2 * TOK + 2 * N_SEQ, HEAD_SIZE), jnp.float32),
            pltpu.VMEM((4, TOK, HEAD_SIZE), jnp.float32),
            pltpu.VMEM((2 * GROUP, TOK, 2 * HEAD_SIZE), jnp.float32),
            pltpu.VMEM((2 * GROUP, TOK, HEAD_SIZE), jnp.float32),
            dma(()), dma((KV_HERE, 2)), dma((KV_HERE,)), dma((KV_HERE, WIDTH // TILE)), dma(()),
            dma(()), dma(()), dma((UNITS, 6)), dma((UNITS, 5)), dma((CHUNKS,)), dma((CHUNKS,)),
        ],
        compiler_params=pltpu.CompilerParams(
            collective_id=0, has_side_effects=True, vmem_limit_bytes=52 << 20
        ),
        name="layer",
    )(input_rows, doc_lengths, w_query.reshape(WIDTH // TILE, TILE, -1), key_weight, value_weight, w_out, table)


def solution(mesh):
    in_specs = (
        P(("seq", "head"), None),
        P(),
        P(None, "head"),
        P(None, "head"),
        P(None, "head"),
        P("head", None),
    )
    out_specs = P(("seq", "head"), None)
    return jax.shard_map(body, mesh=mesh, in_specs=in_specs, out_specs=out_specs, check_vma=False)
```

```python
import math

import jax
import jax.numpy as jnp
import numpy as np
from jax import lax
from jax.experimental import pallas as pl
from jax.experimental.pallas import tpu as pltpu
from jax.sharding import PartitionSpec as P

MESH = pl.DeviceIdType.MESH
HEAD_SIZE = 128
TOK = 256
HALF = 128
WIDTH = 4096
KV_HERE = 4
GROUP = 4
SLOTS = 5
X_RING = 4
N_SEQ = 128
DOCS = 64
NEG_FILL = -1e30
COLS = 1024
CHUNKS = WIDTH // COLS
TILE = GROUP * HEAD_SIZE
PLACES = 6
WIDE_COLS = 2048

UNITS = 2 * KV_HERE
ORDER = ((0, 0), (0, 1), (1, 0), (1, 1), (0, 2), (1, 2), (0, 3), (1, 3))
KEY, VALUE, BOTH = 0, 1, slice(None)
PLACE_OF = (0, 1, 4, 2, 3)
EARLY = 4 * TOK
AT4, AT1, AT3, AT2K, AT2V = range(5)
TO4, TO1, TO3, STRAIGHT, ON_RIGHT, ON_LEFT = range(6)


def inverse_frequency():
    table = []
    for number in range(HEAD_SIZE // 2):
        base_freq = 500000.0 ** (-(2.0 * number) / HEAD_SIZE)
        wavelength = 2.0 * math.pi / base_freq
        smooth = (8192.0 / wavelength - 1.0) / 3.0
        if wavelength < 2048.0:
            table.append(base_freq)
        elif wavelength > 8192.0:
            table.append(base_freq / 8.0)
        else:
            table.append((1.0 - smooth) * base_freq / 8.0 + smooth * base_freq)
    return np.asarray(table, dtype=np.float32).astype(np.float64)


def rotary_tables():
    freq = np.concatenate([inverse_frequency()] * 2)
    rows = np.arange(TOK)[:, None] * freq
    starts = (np.arange(N_SEQ) * TOK)[:, None] * freq
    return np.concatenate(
        [np.cos(rows), np.sin(rows), np.cos(starts), np.sin(starts)]
    ).astype(np.float32)


def kernel(
    x_hbm, docs, wq_hbm, wk_hbm, wv_hbm, wo_hbm, tab_hbm,
    out,
    x, wkv, weights, q, kv, acc, send, recv, att, bias, tab, rope, partial, top,
    x_sem, wkv_sem, wq_sem, wo_sem, tab_sem,
    xs_sem, xr_sem, kv_send, kv_recv, red_send, red_recv,
):
    seq = lax.axis_index("seq")
    head = lax.axis_index("head")
    other = 1 - head
    place = lax.rem(seq, X_RING)
    right = jnp.where(place == X_RING - 1, seq - (X_RING - 1), seq + 1)
    left = jnp.where(place == 0, seq + (X_RING - 1), seq - 1)
    first = place == 0
    last = place == X_RING - 1
    low = place < X_RING // 2
    far = jnp.where(low, seq + 2, seq - 2)
    has_later = seq < N_SEQ - X_RING
    has_earlier = seq >= X_RING
    later = jnp.where(has_later, seq + X_RING, seq)
    earlier = jnp.where(has_earlier, seq - X_RING, seq)
    own_rows = pl.ds(pl.multiple_of(head * HALF, HALF), HALF)
    other_rows = pl.ds(pl.multiple_of(other * HALF, HALF), HALF)

    x_copy = pltpu.make_async_copy(x_hbm, x.at[own_rows, :], x_sem)
    tab_copy = pltpu.make_async_copy(tab_hbm, tab, tab_sem)

    def lanes(number, size):
        return pl.ds(pl.multiple_of(number * size, size), size)

    def wkv_copies(h):
        return (
            pltpu.make_async_copy(
                wk_hbm.at[:, lanes(h, HEAD_SIZE)], wkv.at[h, :, pl.ds(0, HEAD_SIZE)], wkv_sem.at[h, 0]
            ),
            pltpu.make_async_copy(
                wv_hbm.at[:, lanes(h, HEAD_SIZE)],
                wkv.at[h, :, pl.ds(HEAD_SIZE, HEAD_SIZE)],
                wkv_sem.at[h, 1],
            ),
        )

    def wq_copy(h):
        return pltpu.make_async_copy(
            wq_hbm.at[:, :, lanes(h, TILE)], weights.at[h], wq_sem.at[h]
        )

    def wo_place(h):
        return lax.rem(h + KV_HERE, PLACES)

    def wo_copies(h):
        return [
            pltpu.make_async_copy(
                wo_hbm.at[lanes(h, TILE), pl.ds(block * TILE, TILE)],
                weights.at[wo_place(h), block], wo_sem.at[h, block],
            )
            for block in range(WIDTH // TILE)
        ]

    def start_all(copies):
        for copy in copies:
            copy.start()

    def wait_all(copies):
        for copy in copies:
            copy.wait()

    def projected_out(h, first_block, blocks):
        place = wo_place(h)
        return [
            jnp.dot(att[...], weights[place, first_block + block], preferred_element_type=jnp.float32)
            for block in range(blocks)
        ]

    x_copy.start()
    tab_copy.start()
    for h in range(KV_HERE):
        for copy in wkv_copies(h):
            copy.start()

    barrier = pltpu.get_barrier_semaphore()

    def greet(target):
        pl.semaphore_signal(barrier, inc=1, device_id=target, device_id_type=MESH)

    for target in ((seq, other), (right, head), (left, head), (far, head)):
        greet(target)

    @pl.when(has_later)
    def _():
        greet((later, head))

    @pl.when(has_earlier)
    def _():
        greet((earlier, head))

    def x_exchange():
        return pltpu.make_async_remote_copy(
            src_ref=x_hbm,
            dst_ref=x.at[own_rows, :],
            send_sem=xs_sem,
            recv_sem=xr_sem,
            device_id=(seq, other),
            device_id_type=MESH,
        )

    lane = lax.broadcasted_iota(jnp.int32, (TOK, HEAD_SIZE), 1)
    row = lax.broadcasted_iota(jnp.int32, (TOK, HEAD_SIZE), 0)

    tab_copy.wait()
    cos_row, sin_row = tab[pl.ds(0, TOK), :], tab[pl.ds(TOK, TOK), :]
    cos_base = tab[pl.ds(2 * TOK + seq, 1), :]
    sin_base = tab[pl.ds(2 * TOK + N_SEQ + seq, 1), :]
    cosine = cos_row * cos_base - sin_row * sin_base
    sine = sin_row * cos_base + cos_row * sin_base
    sine = jnp.where(lane < HEAD_SIZE // 2, -sine, sine)
    scale = HEAD_SIZE ** (-0.5) * math.log2(math.e)
    rope[0] = cosine
    rope[1] = sine
    rope[2] = cosine * scale
    rope[3] = sine * scale

    def rotated(value, which, rows):
        turned = pltpu.roll(value, HEAD_SIZE // 2, 1)
        return (value * rope[which, rows] + turned * rope[which + 1, rows]).astype(jnp.bfloat16)

    def unit_rows(half, slot):
        core = head if half == 0 else other
        return pl.ds(pl.multiple_of(PLACE_OF[slot] * TOK + core * HALF, HALF), HALF)

    def remote(unit, parts, source, target, leaving, landing, device):
        half, h = unit
        return pltpu.make_async_remote_copy(
            src_ref=kv.at[parts, h, unit_rows(half, source), :],
            dst_ref=kv.at[parts, h, unit_rows(half, target), :],
            send_sem=kv_send.at[half * KV_HERE + h, leaving],
            recv_sem=kv_recv.at[half * KV_HERE + h, landing],
            device_id=(device, head),
            device_id_type=MESH,
        )

    def landed(unit, landing):
        parts = (BOTH, BOTH, BOTH, KEY, VALUE)[landing]
        slot = (4, 1, 3, 2, 2)[landing]
        remote(unit, parts, slot, slot, TO4, landing, right).wait_recv()

    def send_own(half, h):
        unit = (half, h)

        @pl.when(has_later)
        def _():
            remote(unit, BOTH, 0, 4, TO4, AT4, later).start()

        @pl.when(jnp.logical_not(last))
        def _():
            remote(unit, BOTH, 0, 1, TO1, AT1, right).start()

        @pl.when(first)
        def _():
            remote(unit, BOTH, 0, 3, TO3, AT3, left).start()

        @pl.when(place == 1)
        def _():
            remote(unit, KEY, 0, 2, STRAIGHT, AT2K, far).start()

    def pass_on(number):
        unit = ORDER[number]

        @pl.when(has_earlier)
        def _():
            landed(unit, AT4)

        @pl.when(jnp.logical_not(first))
        def _():
            remote(unit, BOTH, 4, 3, TO3, AT3, left).start()

        @pl.when(last)
        def _():
            remote(unit, BOTH, 4, 1, TO1, AT1, right).start()

        @pl.when(place == 2)
        def _():
            remote(unit, KEY, 4, 2, STRAIGHT, AT2K, far).start()

    def pass_own_row(unit):
        @pl.when(last)
        def _():
            landed(unit, AT3)
            remote(unit, VALUE, 3, 2, ON_LEFT, AT2V, left).start()

        @pl.when((place == 1) | (place == 2))
        def _():
            landed(unit, AT1)

            @pl.when(place == 1)
            def _():
                remote(unit, KEY, 1, 2, ON_RIGHT, AT2K, right).start()

            @pl.when(place == 2)
            def _():
                remote(unit, VALUE, 1, 2, ON_RIGHT, AT2V, right).start()

    def pass_far(number):
        unit = ORDER[number]

        @pl.when(first)
        def _():
            landed(unit, AT1)
            remote(unit, KEY, 1, 2, ON_RIGHT, AT2K, right).start()

        @pl.when((place == 1) | (place == 2))
        def _():
            landed(unit, AT3)
            remote(unit, VALUE, 3, 2, ON_LEFT, AT2V, left).start()

        pass_own_row(unit)

    def project_kv(half, h):
        rows = own_rows if half == 0 else other_rows
        both = jnp.dot(x[rows, :], wkv[h], preferred_element_type=jnp.float32)
        kv[0, h, unit_rows(half, 0), :] = rotated(both[:, :HEAD_SIZE], 0, rows)
        kv[1, h, unit_rows(half, 0), :] = both[:, HEAD_SIZE:].astype(jnp.bfloat16)

    def project_own(h, carry):
        for copy in wkv_copies(h):
            copy.wait()
        wq_copy(h).start()
        project_kv(0, h)
        return carry

    x_copy.wait()
    lax.fori_loop(0, 2, project_own, 0)

    callers = 4 + has_later.astype(jnp.int32) + has_earlier.astype(jnp.int32)
    pl.semaphore_wait(barrier, callers)
    x_exchange().start()
    send_own(0, 0)
    send_own(0, 1)
    lax.fori_loop(2, KV_HERE, project_own, 0)

    base = seq * TOK
    position = base + lax.broadcasted_iota(jnp.int32, (8, TOK), 1)

    def next_doc(number, state):
        end, start = state
        end = end + docs[number]
        return end, jnp.where(end <= position, end, start)

    _, start_row = lax.fori_loop(
        0, DOCS, next_doc, (jnp.int32(0), jnp.zeros((8, TOK), jnp.int32))
    )
    start_row = start_row.astype(jnp.float32)
    start = jnp.transpose(jnp.concatenate([start_row] * (HEAD_SIZE // 8), axis=0))
    base_f = base.astype(jnp.float32)
    for slot in range(SLOTS):
        for half in range(TOK // HEAD_SIZE):
            offset = lane + half * HEAD_SIZE
            allowed = offset.astype(jnp.float32) + (base_f - float(slot * TOK)) >= start
            if slot == 0:
                allowed = allowed & (offset <= row)
            bias[:, pl.ds(PLACE_OF[slot] * TOK + half * HEAD_SIZE, HEAD_SIZE)] = jnp.where(
                allowed, 0.0, NEG_FILL
            )

    @pl.when(jnp.logical_not(has_earlier))
    def _():
        kv[:, :, pl.ds(PLACE_OF[4] * TOK, TOK), :] = jnp.zeros((2, KV_HERE, TOK, HEAD_SIZE), jnp.bfloat16)

    acc[...] = jnp.zeros_like(acc)
    x_exchange().wait()

    def project_other(h, carry):
        @pl.when(h >= 2)
        def _():
            send_own(0, h)

        project_kv(1, h)
        send_own(1, h)
        return carry

    lax.fori_loop(0, KV_HERE, project_other, 0)
    pass_on(0)
    after_query = (
        lambda: pass_on(1),
        lambda: pass_on(2),
        lambda: (pass_on(3), pass_far(0)),
        lambda: (pass_on(4), pass_far(1)),
    )

    def project_q(h, carry):
        @pl.when(h < PLACES - KV_HERE)
        def _():
            start_all(wo_copies(h))

        wq_copy(h).wait()
        columns = weights[h].reshape(WIDTH, TILE)
        some = jnp.dot(x[...], columns, preferred_element_type=jnp.float32)
        for number in range(GROUP):
            q[h * GROUP + number] = rotated(
                some[:, number * HEAD_SIZE : (number + 1) * HEAD_SIZE], 2, slice(None)
            )

        @pl.when(h < 2 * KV_HERE - PLACES)
        def _():
            start_all(wo_copies(h + PLACES - KV_HERE))

        for step, actions in enumerate(after_query):
            @pl.when(h == step)
            def _():
                actions()

        return carry

    lax.fori_loop(0, KV_HERE, project_q, 0)
    def reduce_copy(chunk):
        return pltpu.make_async_remote_copy(
            src_ref=send.at[chunk],
            dst_ref=recv.at[chunk],
            send_sem=red_send.at[chunk],
            recv_sem=red_recv.at[chunk],
            device_id=(seq, other),
            device_id_type=MESH,
        )

    def values_of(h, rows):
        values = kv[VALUE, h, rows, :]
        return jnp.concatenate([values, jnp.ones_like(values)], axis=1)

    def scores_of(h, number, rows):
        score = lax.dot_general(
            q[h * GROUP + number], kv[KEY, h, rows, :], (((1,), (1,)), ((), ())),
            preferred_element_type=jnp.float32,
        )
        return score + bias[:, rows]

    def attend_early(h):
        for half in range(2):
            @pl.when(last)
            def _():
                landed((half, h), AT1)

            @pl.when(first)
            def _():
                landed((half, h), AT3)

        rows = slice(0, EARLY)
        values = values_of(h, rows)
        for number in range(GROUP):
            score = scores_of(h, number, rows)
            rowmax = jnp.max(score, axis=1, keepdims=True)
            weight = jnp.exp2(score - rowmax).astype(jnp.bfloat16)
            kept = lax.rem(h, 2) * GROUP + number
            partial[kept] = jnp.dot(weight, values, preferred_element_type=jnp.float32)
            top[kept] = jnp.broadcast_to(rowmax, (TOK, HEAD_SIZE))

    def attend_late(h):
        for half in range(2):
            landed((half, h), AT2K)
            landed((half, h), AT2V)

        rows = slice(EARLY, SLOTS * TOK)
        values = values_of(h, rows)
        for number in range(GROUP):
            kept = lax.rem(h, 2) * GROUP + number
            score = scores_of(h, number, rows)
            before = top[kept]
            rowmax = jnp.maximum(before, jnp.max(score, axis=1, keepdims=True))
            factor = jnp.exp2(before - rowmax)
            weight = jnp.exp2(score - jnp.concatenate([rowmax, rowmax], axis=1))
            mixed = jnp.dot(weight.astype(jnp.bfloat16), values, preferred_element_type=jnp.float32)
            mixed = mixed + partial[kept] * jnp.concatenate([factor, factor], axis=1)
            att[:, number * HEAD_SIZE : (number + 1) * HEAD_SIZE] = (
                mixed[:, :HEAD_SIZE] / mixed[:, HEAD_SIZE:]
            ).astype(jnp.bfloat16)

    def project_out(h):
        wait_all(wo_copies(h))

        def some(chunk, carry):
            blocks = WIDE_COLS // TILE
            for block, sums in enumerate(projected_out(h, chunk * blocks, blocks)):
                acc[:, lanes(chunk * blocks + block, TILE)] += sums
            return carry

        lax.fori_loop(0, WIDTH // WIDE_COLS, some, 0)

    def attend(step, carry):
        def at(number, *actions):
            @pl.when(step == number)
            def _():
                for action, unit in actions:
                    action(unit)

        at(0, (pass_on, 5), (pass_far, 2))
        at(1, (pass_on, 6), (pass_far, 3))
        at(2, (pass_far, 5))

        @pl.when(step < KV_HERE)
        def _():
            attend_early(step)

        at(1, (pass_on, 7), (pass_far, 4))
        at(2, (pass_far, 6))

        @pl.when(step >= 1)
        def _():
            attend_late(step - 1)

        at(2, (pass_far, 7))

        @pl.when((step >= 1) & (step < KV_HERE))
        def _():
            project_out(step - 1)

        return carry

    lax.fori_loop(0, KV_HERE + 1, attend, 0)
    wait_all(wo_copies(KV_HERE - 1))

    def project_last(chunk, carry):
        columns = lanes(chunk, COLS)
        blocks = COLS // TILE
        for block, sums in enumerate(projected_out(KV_HERE - 1, chunk * blocks, blocks)):
            acc[:, lanes(chunk * blocks + block, TILE)] += sums
        send[chunk] = acc[other_rows, columns].astype(jnp.bfloat16)
        reduce_copy(chunk).start()
        return carry

    lax.fori_loop(0, CHUNKS, project_last, 0)

    def sent(h, carry):
        for half in range(2):
            def gone(parts, leaving):
                remote((half, h), parts, 0, 0, leaving, AT4, right).wait_send()

            gone(BOTH, TO1)
            gone(BOTH, TO3)

            @pl.when(has_later)
            def _():
                gone(BOTH, TO4)

            @pl.when((place == 1) | (place == 2))
            def _():
                gone(KEY, STRAIGHT)

            @pl.when(jnp.logical_not(last))
            def _():
                gone(KEY, ON_RIGHT)

            @pl.when(jnp.logical_not(first))
            def _():
                gone(VALUE, ON_LEFT)

        return carry

    lax.fori_loop(0, KV_HERE, sent, 0)

    def finish(chunk, carry):
        columns = lanes(chunk, COLS)
        reduce_copy(chunk).wait()
        out[:, columns] = (
            acc[own_rows, columns] + recv[chunk].astype(jnp.float32)
        ).astype(jnp.bfloat16)
        return carry

    lax.fori_loop(0, CHUNKS, finish, 0)


def body(input_rows, doc_lengths, w_query, key_weight, value_weight, w_out):
    table = jnp.asarray(rotary_tables())
    hbm = pl.BlockSpec(memory_space=pl.ANY)
    dma = pltpu.SemaphoreType.DMA
    wide = GROUP * HEAD_SIZE
    return pl.pallas_call(
        kernel,
        out_shape=jax.ShapeDtypeStruct((HALF, WIDTH), jnp.bfloat16),
        in_specs=[hbm, pl.BlockSpec(memory_space=pltpu.SMEM), hbm, hbm, hbm, hbm, hbm],
        out_specs=pl.BlockSpec(memory_space=pltpu.VMEM),
        scratch_shapes=[
            pltpu.VMEM((TOK, WIDTH), jnp.bfloat16),
            pltpu.VMEM((KV_HERE, WIDTH, 2 * HEAD_SIZE), jnp.bfloat16),
            pltpu.VMEM((PLACES, WIDTH // TILE, TILE, TILE), jnp.bfloat16),
            pltpu.VMEM((KV_HERE * GROUP, TOK, HEAD_SIZE), jnp.bfloat16),
            pltpu.VMEM((2, KV_HERE, SLOTS * TOK, HEAD_SIZE), jnp.bfloat16),
            pltpu.VMEM((TOK, WIDTH), jnp.float32),
            pltpu.VMEM((CHUNKS, HALF, COLS), jnp.bfloat16),
            pltpu.VMEM((CHUNKS, HALF, COLS), jnp.bfloat16),
            pltpu.VMEM((TOK, wide), jnp.bfloat16),
            pltpu.VMEM((TOK, SLOTS * TOK), jnp.float32),
            pltpu.VMEM((2 * TOK + 2 * N_SEQ, HEAD_SIZE), jnp.float32),
            pltpu.VMEM((4, TOK, HEAD_SIZE), jnp.float32),
            pltpu.VMEM((2 * GROUP, TOK, 2 * HEAD_SIZE), jnp.float32),
            pltpu.VMEM((2 * GROUP, TOK, HEAD_SIZE), jnp.float32),
            dma(()), dma((KV_HERE, 2)), dma((KV_HERE,)), dma((KV_HERE, WIDTH // TILE)), dma(()),
            dma(()), dma(()), dma((UNITS, 6)), dma((UNITS, 5)), dma((CHUNKS,)), dma((CHUNKS,)),
        ],
        compiler_params=pltpu.CompilerParams(
            collective_id=0, has_side_effects=True, vmem_limit_bytes=52 << 20
        ),
        name="layer",
    )(input_rows, doc_lengths, w_query.reshape(WIDTH // TILE, TILE, -1), key_weight, value_weight, w_out, table)


def solution(mesh):
    in_specs = (
        P(("seq", "head"), None),
        P(),
        P(None, "head"),
        P(None, "head"),
        P(None, "head"),
        P("head", None),
    )
    out_specs = P(("seq", "head"), None)
    return jax.shard_map(body, mesh=mesh, in_specs=in_specs, out_specs=out_specs, check_vma=False)
```
